32 devices in a mesh: dp: 8 (over z, y), tp: 4 (over x, core).
Axes of the slice: x: 2, y: 2, z: 4, core: 2. Of those that a mesh axis runs over, the one named last changes fastest.
Arguments:
- tokens: bfloat16 [16, 1536, 768], P('dp'), may hold values from -6 to 6
- cube_lengths: int32 [16], P('dp'), may hold values from 864 to 1536, as said below
- query_weight: bfloat16 [768, 768], P(None, 'tp'), may hold values from -0.3125 to 0.3125
- query_bias: bfloat16 [768], P('tp'), may hold values from -3 to 3
- key_weight: bfloat16 [768, 768], P(None, 'tp'), may hold values from -0.3125 to 0.3125
- value_weight: bfloat16 [768, 768], P(None, 'tp'), may hold values from -0.21875 to 0.21875
- value_bias: bfloat16 [768], P('tp'), may hold values from -2 to 2
- out_weight: bfloat16 [768, 768], P('tp'), may hold values from -0.875 to 0.875
- out_bias: bfloat16 [768], replicated, may hold values from -2 to 2
- first_gain: bfloat16 [768], replicated, may hold values from 0.5 to 1.5
- first_shift: bfloat16 [768], replicated, may hold values from -2 to 2
- second_gain: bfloat16 [768], replicated, may hold values from 0.5 to 1.5
- second_shift: bfloat16 [768], replicated, may hold values from -2 to 2
- up_weight: bfloat16 [768, 3072], P(None, 'tp'), may hold values from -0.21875 to 0.21875
- up_bias: bfloat16 [3072], P('tp'), may hold values from -3 to 3
- down_weight: bfloat16 [3072, 768], P('tp'), may hold values from -0.109375 to 0.109375
- down_bias: bfloat16 [768], replicated, may hold values from -2 to 2
- cotangent: bfloat16 [16, 1536, 768], P('dp'), may hold values from -6 to 6
Outputs:
- output: bfloat16 [16, 1536, 768], P('dp')
- input_grad: bfloat16 [16, 1536, 768], P('dp')
- query_weight_grad: float32 [768, 768], P(None, 'tp')
- query_bias_grad: float32 [768], P('tp')
- key_weight_grad: float32 [768, 768], P(None, 'tp')
- value_weight_grad: float32 [768, 768], P(None, 'tp')
- value_bias_grad: float32 [768], P('tp')
- out_weight_grad: float32 [768, 768], P('tp')
- out_bias_grad: float32 [768], replicated
- first_gain_grad: float32 [768], replicated
- first_shift_grad: float32 [768], replicated
- second_gain_grad: float32 [768], replicated
- second_shift_grad: float32 [768], replicated
- up_weight_grad: float32 [768, 3072], P(None, 'tp')
- up_bias_grad: float32 [3072], P('tp')
- down_weight_grad: float32 [3072, 768], P('tp')
- down_bias_grad: float32 [768], replicated
The draws below stay inside these ranges and needn't reach their ends.
Inputs may be any that keep to these rules, and one draw needn't show every extreme that they name: `cube_lengths`: each cube holds 1536 or 864 tokens; both lengths occur in every draw.
All inputs are finite; a program needn't handle non-finite values.
Results may differ from the reference program's by a relative error of at most 0.02.
Values may be sent and summed in bfloat16 or wider, within the bound.
No kernel may reach another device: no remote copies, remote signals or barrier semaphores. Data moves between devices by JAX's collectives and lax.ppermute only.
A program may use at most 256 MiB of HBM per device.

```python
from functools import partial
import jax
import jax.numpy as jnp
from jax import lax

D = 768
HEADS = 12
HEAD_DIM = 64
FF = 3072
LMAX = 1536
CUBE_SHORT = 864
CUBES = 16
N_TP = 4


def draw_cube_lengths(key, part):
    picks = jax.random.randint(key, (CUBES,), 0, 2)
    picks = picks.at[0].set(1).at[1].set(0)
    return (CUBE_SHORT + (LMAX - CUBE_SHORT) * picks).astype(jnp.int32)


def block_scale(own_key, shape, shards, smallest, high):
    loudness = 1.0
    for axis_at, blocks in shards:
        steps = jax.random.uniform(jax.random.fold_in(jax.random.fold_in(own_key, 6), axis_at), (blocks,), jnp.float32, smallest / len(shards), high / len(shards))
        loudness = loudness * jnp.repeat(jnp.exp(steps), shape[axis_at] // blocks).reshape((-1,) + (1,) * (len(shape) - 1 - axis_at))
    return loudness


def bell_draw(rng, extent, scale, bound, shards=(), held_as=jnp.bfloat16):
    values = scale * jax.random.normal(rng, extent, jnp.float32)
    if shards:
        values = values * block_scale(rng, extent, shards, -0.22, 0.18)
    return jnp.clip(values, -bound, bound).astype(held_as)


def setup_inputs(seed: int = 0) -> dict:
    key_of = jax.random.split(jax.random.key(seed), 19)
    tokens = bell_draw(key_of[0], (CUBES, LMAX, D), 1.0, 6.0, ((0, 8),))
    cube_lengths = draw_cube_lengths(jax.random.fold_in(key_of[18], 71), 0)
    query_weight = bell_draw(key_of[2], (D, D), (D // 2) ** -0.5, 0.3125, ((1, 4),))
    query_bias = bell_draw(key_of[3], (D,), 0.5, 3.0, ((0, 4),))
    key_weight = bell_draw(key_of[4], (D, D), (D // 2) ** -0.5, 0.3125, ((1, 4),))
    value_weight = bell_draw(key_of[5], (D, D), D ** -0.5, 0.21875, ((1, 4),))
    value_bias = bell_draw(key_of[6], (D,), 0.3, 2.0, ((0, 4),))
    out_weight = bell_draw(key_of[7], (D, D), (D // 16) ** -0.5, 0.875, ((0, 4),))
    out_bias = bell_draw(key_of[8], (D,), 0.3, 2.0)
    first_gain = jnp.clip(1.0 + 0.1 * jax.random.normal(key_of[9], (D,), jnp.float32), 0.5, 1.5).astype(jnp.bfloat16)
    first_shift = bell_draw(key_of[10], (D,), 0.3, 2.0)
    second_gain = jnp.clip(1.0 + 0.1 * jax.random.normal(key_of[11], (D,), jnp.float32), 0.5, 1.5).astype(jnp.bfloat16)
    second_shift = bell_draw(key_of[12], (D,), 0.3, 2.0)
    up_weight = bell_draw(key_of[13], (D, FF), D ** -0.5, 0.21875, ((1, 4),))
    up_bias = bell_draw(key_of[14], (FF,), 0.5, 3.0, ((0, 4),))
    down_weight = bell_draw(key_of[15], (FF, D), FF ** -0.5, 0.109375, ((0, 4),))
    down_bias = bell_draw(key_of[16], (D,), 0.3, 2.0)
    cotangent = bell_draw(key_of[17], (CUBES, LMAX, D), 1.0, 6.0, ((0, 8),))
    return dict(tokens=tokens, cube_lengths=cube_lengths, query_weight=query_weight, query_bias=query_bias, key_weight=key_weight, value_weight=value_weight, value_bias=value_bias, out_weight=out_weight, out_bias=out_bias, first_gain=first_gain, first_shift=first_shift, second_gain=second_gain, second_shift=second_shift, up_weight=up_weight, up_bias=up_bias, down_weight=down_weight, down_bias=down_bias, cotangent=cotangent)


@jax.custom_vjp
def low(v):
    return lax.optimization_barrier(v.astype(jnp.bfloat16)).astype(jnp.float32)

@jax.custom_vjp
def low_back(v):
    return v

def low_keep(v):
    return (low(v), None)

def low_pass(kept, grad):
    return (grad,)

def back_keep(v):
    return (v, None)

def back_low(kept, grad):
    return (low(grad),)
low.defvjp(low_keep, low_pass)
low_back.defvjp(back_keep, back_low)
epsilon = 1e-06
masked_score = -1e+30

def layer_norm(values, gain, shift):
    center = values - lax.optimization_barrier(jnp.mean(values, -1, keepdims=True))
    spread = lax.optimization_barrier(jnp.mean(center * center, -1, keepdims=True))
    return center * lax.rsqrt(spread + epsilon) * gain + shift

def project(left, right):
    return jnp.einsum('cld,de->cle', left, right, precision=lax.Precision.HIGHEST)

def attend_cube(inputs):
    query, keys, values, length = inputs
    scores = low_back(jnp.einsum('qhd,khd->hqk', query, keys, precision=lax.Precision.HIGHEST) * HEAD_DIM ** (-0.5))
    position = lax.broadcasted_iota(jnp.int32, scores.shape, 2)
    scores = jnp.where(position < length, scores, masked_score)
    probs = low(jax.nn.softmax(scores, axis=-1))
    return jnp.einsum('hqk,khd->qhd', probs, values, precision=lax.Precision.HIGHEST)

def forward(lengths, tokens, query_weight, query_bias, key_weight, value_weight, value_bias, out_weight, out_bias, first_gain, first_shift, second_gain, second_shift, up_weight, up_bias, down_weight, down_bias):
    cubes = tokens.shape[0]
    width = D // N_TP
    hidden_width = FF // N_TP
    group_heads = HEADS // N_TP
    normed = low(layer_norm(tokens, first_gain, first_shift))
    branch = jnp.zeros_like(tokens)
    for shard_index in range(N_TP):
        columns = slice(shard_index * width, (shard_index + 1) * width)
        shared = low_back(normed)
        query = low(low_back(project(shared, query_weight[:, columns]) + query_bias[columns]))
        keys = low(low_back(project(shared, key_weight[:, columns])))
        values = low(low_back(project(shared, value_weight[:, columns]) + value_bias[columns]))
        shape = (cubes, LMAX, group_heads, HEAD_DIM)
        attended = lax.map(jax.checkpoint(attend_cube), (query.reshape(shape), keys.reshape(shape), values.reshape(shape), lengths))
        mixed = low(low_back(attended.reshape(cubes, LMAX, width)))
        branch = branch + low(project(mixed, out_weight[columns, :]))
    middle = tokens + low_back(branch + out_bias)
    normed_two = low(layer_norm(middle, second_gain, second_shift))
    feed = jnp.zeros_like(tokens)
    for shard_index in range(N_TP):
        columns = slice(shard_index * hidden_width, (shard_index + 1) * hidden_width)
        shared = low_back(normed_two)
        upper = low_back(project(shared, up_weight[:, columns]) + up_bias[columns])
        active = low(jax.nn.gelu(upper, approximate=False))
        feed = feed + low(project(active, down_weight[columns, :]))
    return middle + low_back(feed + down_bias)

def reference(tokens, cube_lengths, query_weight, query_bias, key_weight, value_weight, value_bias, out_weight, out_bias, first_gain, first_shift, second_gain, second_shift, up_weight, up_bias, down_weight, down_bias, cotangent):
    floats = [array.astype(jnp.float32) for array in (tokens, query_weight, query_bias, key_weight, value_weight, value_bias, out_weight, out_bias, first_gain, first_shift, second_gain, second_shift, up_weight, up_bias, down_weight, down_bias)]
    valid = (lax.broadcasted_iota(jnp.int32, (CUBES, LMAX), 1) < cube_lengths[:, None]).astype(jnp.float32)
    output, pullback = jax.vjp(partial(forward, cube_lengths), *floats)
    grads = pullback(cotangent.astype(jnp.float32) * valid[:, :, None])
    return (output.astype(jnp.bfloat16), grads[0].astype(jnp.bfloat16), grads[1], grads[2], grads[3], grads[4], grads[5], grads[6], grads[7], grads[8], grads[9], grads[10], grads[11], grads[12], grads[13], grads[14], grads[15])
```

```python
from functools import partial

import jax
import jax.numpy as jnp
from jax import lax
from jax.experimental import pallas as pl
from jax.experimental.pallas import tpu as pltpu
from jax.sharding import PartitionSpec as P

HEAD_DIM = 64
SHORT = 864
ROWS = 256
LANES = 128
WIDE = 256
EPS = 1e-06
LOG2E = 1.4426950408889634
LN2 = 0.6931471805599453
BF16 = jnp.bfloat16
F32 = jnp.float32

NN = (((1,), (0,)), ((), ()))
NT = (((1,), (1,)), ((), ()))
TN = (((0,), (0,)), ((), ()))


def dot(left, right, dims):
    return lax.dot_general(left, right, dims, preferred_element_type=F32)


def shape_of(shape, dtype):
    return jax.ShapeDtypeStruct(shape, dtype)


def run(body, scalars, grid, in_specs, out_specs, out_shape, scratch=(), flops=0, name=None):
    def call(*arrays):
        moved = sum(a.size * a.dtype.itemsize for a in arrays)
        moved += sum(s.size * s.dtype.itemsize for s in out_shape)
        return pl.pallas_call(
            body,
            grid_spec=pltpu.PrefetchScalarGridSpec(
                num_scalar_prefetch=1,
                grid=grid,
                in_specs=in_specs,
                out_specs=out_specs,
                scratch_shapes=list(scratch),
            ),
            out_shape=out_shape,
            compiler_params=pltpu.CompilerParams(vmem_limit_bytes=58 << 20),
            cost_estimate=pl.CostEstimate(
                flops=int(flops), transcendentals=0, bytes_accessed=int(moved)
            ),
            name=name,
        )(scalars, *arrays)

    return call


def whole(shape):
    return pl.BlockSpec(shape, lambda i, s: (0,) * len(shape))


def rows_of(width):
    return pl.BlockSpec((ROWS, width), lambda i, s: (i, 0))


def cube_rows(width):
    return pl.BlockSpec((1, ROWS, width), lambda i, s: (s[0], i, 0))


def own_rows(width, blocks):
    return pl.BlockSpec((ROWS, width), lambda i, s: (s[1] * blocks + i, 0))


def normalize(values):
    center = values - jnp.mean(values, -1, keepdims=True)
    inverse = lax.rsqrt(jnp.mean(center * center, -1, keepdims=True) + EPS)
    return center * inverse, inverse


def norm_back(grad, normal, inverse, gain):
    scaled = grad * gain
    return inverse * (
        scaled
        - jnp.mean(scaled, -1, keepdims=True)
        - normal * jnp.mean(scaled * normal, -1, keepdims=True)
    )


def column_sums(values):
    return jnp.sum(values, 0, keepdims=True)


def sum_rows(values):
    return dot(jnp.ones((8, values.shape[0]), BF16), values, NN)[0:1]


def accumulate(ref, value):
    first = pl.program_id(0) == 0

    @pl.when(first)
    def _():
        ref[...] = value

    @pl.when(jnp.logical_not(first))
    def _():
        ref[...] += value


def scale_query(qkv):
    query = qkv[:, :WIDE] * (HEAD_DIM**-0.5 * LOG2E)
    return query.astype(BF16), qkv[:, WIDE:].astype(BF16)


def first_body(s, tokens, gain, shift, weight, bias, normed_out, qkv_out):
    normal, _ = normalize(tokens[0].astype(F32))
    normed = (normal * gain[...].astype(F32) + shift[...].astype(F32)).astype(BF16)
    normed_out[...] = normed
    qkv = dot(normed, weight[...], NN) + bias[...].astype(F32)
    qkv_out[:, :WIDE], qkv_out[:, WIDE:] = scale_query(qkv)


def project_body(s, normed, weight, bias, qkv_out):
    qkv = dot(normed[...], weight[...], NN) + bias[...].astype(F32)
    qkv_out[:, :WIDE], qkv_out[:, WIDE:] = scale_query(qkv)


def head_view(ref, rows, base, head):
    lane = lax.broadcasted_iota(jnp.int32, (1, LANES), 1)
    if head == 2:
        return ref[rows, base + LANES : base + 2 * LANES]
    keep = (lane < HEAD_DIM) if head == 0 else (lane >= HEAD_DIM)
    return jnp.where(keep, ref[rows, base : base + LANES], jnp.zeros((), BF16))


def pair_view(ref, rows, base, head):
    start = base + (LANES if head == 2 else 0)
    return ref[rows, start : start + LANES]


def attend_part(query, keys_values, attended, logsum, limit, block):
    lane = lax.broadcasted_iota(jnp.int32, (1, LANES), 1)
    count = query.shape[0] // block
    keys = slice(0, limit)

    def scores(unit):
        at, head = unit
        return dot(
            head_view(query, slice(at * block, (at + 1) * block), 0, head),
            pair_view(keys_values, keys, WIDE, head),
            NT,
        )

    units = [(at, head) for at in range(count) for head in range(3)]
    current = scores(units[0])
    done = []
    for index, (at, head) in enumerate(units):
        following = scores(units[index + 1]) if index + 1 < len(units) else None
        peak = jnp.max(current, -1, keepdims=True)
        expo = jnp.exp2(current - peak)
        total = jnp.sum(expo, -1, keepdims=True)
        mixed = dot(expo.astype(BF16), pair_view(keys_values, keys, 2 * WIDE, head), NN)
        done.append((mixed * (1.0 / total), peak + jnp.log2(total)))
        current = following
        if head == 2:
            rows = slice(at * block, (at + 1) * block)
            (one, log_one), (two, log_two), (three, log_three) = done
            attended[rows, :LANES] = jnp.where(lane < HEAD_DIM, one, two).astype(BF16)
            attended[rows, LANES:] = three.astype(BF16)
            table = jnp.where(lane == 0, log_one, jnp.where(lane == 1, log_two, log_three))
            logsum[:, rows] = jnp.transpose(table)[:8]
            done = []


def attend_body(s, query, keys_values, attended, logsum):
    full = keys_values.shape[0]

    @pl.when(s[2] == full)
    def _():
        attend_part(query, keys_values, attended, logsum, full, ROWS)

    @pl.when(s[2] != full)
    def _():
        attend_part(query, keys_values, attended, logsum, SHORT, ROWS)


def attend_back_part(qkv, grad, logsum, inner, grads, heads, limit, block, full):
    lane = lax.broadcasted_iota(jnp.int32, (1, LANES), 1)
    count = -(-limit // block)
    keys = slice(0, limit)

    def front(unit):
        head, at = unit
        rows = slice(at * block, min((at + 1) * block, limit))
        query = head_view(qkv, rows, 0, head)
        pull = head_view(grad, rows, 0, head)
        return (
            dot(pair_view(qkv, keys, WIDE, head), query, NT),
            dot(pair_view(qkv, keys, 2 * WIDE, head), pull, NT),
            query,
            pull,
        )

    def put(rows, base, head, value):
        value = value.astype(BF16)
        start = base + (LANES if head == 2 else 0)
        if head == 1:
            value = jnp.where(lane < HEAD_DIM, grads[rows, start : start + LANES], value)
        grads[rows, start : start + LANES] = value

    units = [(head, at) for head in heads for at in range(count)]
    current = front(units[0])
    for index, (head, at) in enumerate(units):
        following = front(units[index + 1]) if index + 1 < len(units) else None
        scores, grad_probs, query, pull = current
        rows = slice(at * block, min((at + 1) * block, limit))
        probs = jnp.exp2(scores - logsum[head : head + 1, rows])
        grad_scores = (probs * (grad_probs - inner[head : head + 1, rows])).astype(BF16)
        value_part = dot(probs.astype(BF16), pull, NN)
        key_part = dot(grad_scores, query, NN)
        grad_values = value_part if at == 0 else grad_values + value_part
        grad_keys = key_part if at == 0 else grad_keys + key_part
        grad_query = dot(grad_scores, pair_view(qkv, keys, WIDE, head), TN)
        put(rows, 0, head, grad_query * HEAD_DIM**-0.5)
        if at == count - 1:
            put(keys, WIDE, head, grad_keys * LN2)
            put(keys, 2 * WIDE, head, grad_values)
        current = following
    if limit < full:
        grads[limit:, :] = jnp.zeros((full - limit, grads.shape[1]), BF16)


def attend_back_body(s, qkv, grad, logsum, inner, grads):
    full = qkv.shape[0]

    @pl.when(s[2] == full)
    def _():
        attend_back_part(qkv, grad, logsum, inner, grads, (0, 1, 2), full, ROWS, full)

    @pl.when(s[2] != full)
    def _():
        attend_back_part(qkv, grad, logsum, inner, grads, (0, 1, 2), SHORT, ROWS, full)


def middle_body(s, tokens, a0, a1, a2, a3, w0, w1, w2, w3, bias, gain, shift, middle_out, normed_out):
    branch = dot(a0[...], w0[...], NN) + dot(a1[...], w1[...], NN)
    branch += dot(a2[...], w2[...], NN) + dot(a3[...], w3[...], NN)
    middle = tokens[0].astype(F32) + branch + bias[...].astype(F32)
    middle_out[...] = middle
    normal, _ = normalize(middle)
    normed_out[...] = (normal * gain[...].astype(F32) + shift[...].astype(F32)).astype(BF16)


def gelu_and_slope(values):
    t = 1.0 / (1.0 + (0.3275911 * 0.7071067811865476) * jnp.abs(values))
    series = t * (
        0.254829592 + t * (-0.284496736 + t * (1.421413741 + t * (-1.453152027 + t * 1.061405429)))
    )
    decay = jnp.exp2(values * values * (-0.5 * LOG2E))
    tail = 0.5 * series * decay
    share = jnp.where(values >= 0, 1.0 - tail, tail)
    scaled = values * share
    return scaled, share + values * (decay * 0.3989422804014327)


def valid_rows(s, at):
    position = at * ROWS + lax.broadcasted_iota(jnp.int32, (ROWS, 1), 0)
    return position < s[2]


def hidden_body(s, normed, cot, up, down, bias, active_out, upper_out, feed_out, back_out, bias_out):
    at = pl.program_id(0)
    upper = dot(normed[...], up[...], NN) + bias[...].astype(F32)
    grad_feed = jnp.where(valid_rows(s, at), cot[0], jnp.zeros((), BF16))
    grad_active = dot(grad_feed, down[...], NT)
    active, slope = gelu_and_slope(upper)
    active = active.astype(BF16)
    active_out[...] = active
    grad_upper = (grad_active * slope).astype(BF16)
    upper_out[...] = grad_upper
    feed_out[...] = dot(active, down[...], NN).astype(BF16)
    back_out[...] = dot(grad_upper, up[...], NT).astype(BF16)
    accumulate(bias_out, sum_rows(grad_upper))


def hidden_weights_body(s, normed, upper, active, cot, up_out, down_out):
    length, width = normed.shape
    position = lax.broadcasted_iota(jnp.int32, (length, 1), 0)
    grad_feed = jnp.where(position < s[2], cot[0], jnp.zeros((), BF16))
    up_out[...] = dot(normed[...], upper[...], TN).astype(BF16)
    down_out[...] = dot(active[...], grad_feed, TN).astype(BF16)


def back_two_body(
    s, middle, cot, g0, g1, g2, g3, gain, w0, w1, a0, a1,
    grad_out, at0_out, at1_out, in0_out, in1_out, ow0_out, ow1_out, sums_out, acc0, acc1,
):
    at = pl.program_id(0)
    normal, inverse = normalize(middle[...])
    grad_normed = (g0[...].astype(F32) + g1[...].astype(F32)) + (g2[...].astype(F32) + g3[...].astype(F32))
    grad_feed = jnp.where(valid_rows(s, at), cot[0], jnp.zeros((), BF16)).astype(F32)
    grad_middle = grad_feed + norm_back(grad_normed, normal, inverse, gain[...].astype(F32))
    grad_out[...] = grad_middle
    grad_branch = grad_middle.astype(BF16)
    sums = jnp.concatenate(
        [
            column_sums(grad_normed * normal),
            column_sums(grad_normed),
            column_sums(grad_branch.astype(F32)),
            column_sums(grad_feed),
        ],
        0,
    )
    accumulate(sums_out, sums)
    lane = lax.broadcasted_iota(jnp.int32, (8, WIDE), 1)
    head = lax.broadcasted_iota(jnp.int32, (8, WIDE), 0)
    member = (lane // HEAD_DIM == head).astype(BF16)
    for weight, att, at_out, in_out, acc in (
        (w0, a0, at0_out, in0_out, acc0),
        (w1, a1, at1_out, in1_out, acc1),
    ):
        grad_att = dot(grad_branch, weight[...], NT).astype(BF16)
        at_out[...] = grad_att
        product = grad_att.astype(F32) * att[...].astype(F32)
        high = product.astype(BF16)
        low = (product - high.astype(F32)).astype(BF16)
        in_out[...] = dot(member, high, NT) + dot(member, low, NT)
        accumulate(acc, dot(att[...], grad_branch, TN))

    @pl.when(at == pl.num_programs(0) - 1)
    def _():
        ow0_out[...] = acc0[...].astype(BF16)
        ow1_out[...] = acc1[...].astype(BF16)


def qkv_weights_body(s, normed, grads, weight_out, bias_out):
    weight_out[...] = dot(grads[...], normed[...], TN).astype(BF16)
    bias_out[...] = sum_rows(grads[...])


def qkv_back_body(s, grads, weight, back_out):
    back_out[...] = dot(grads[...], weight[...], NT).astype(BF16)


def back_one_body(s, tokens, grad_middle, g0, g1, g2, g3, gain, grad_out, sums_out):
    normal, inverse = normalize(tokens[0].astype(F32))
    grad_normed = (g0[...].astype(F32) + g1[...].astype(F32)) + (g2[...].astype(F32) + g3[...].astype(F32))
    accumulate(
        sums_out, jnp.concatenate([column_sums(grad_normed * normal), column_sums(grad_normed)], 0)
    )
    grad_out[...] = (
        grad_middle[...] + norm_back(grad_normed, normal, inverse, gain[...].astype(F32))
    ).astype(BF16)


def pairs(count, mask):
    return [(i, i ^ mask) for i in range(count)]


def local(
    dp, tp,
    tokens, cube_lengths, query_weight, query_bias, key_weight, value_weight, value_bias,
    out_weight, out_bias, first_gain, first_shift, second_gain, second_shift,
    up_weight, up_bias, down_weight, down_bias, cotangent,
):
    slots, length, width = tokens.shape
    group = query_weight.shape[1]
    hidden = up_weight.shape[1]
    blocks = length // ROWS
    half = length // 2
    half_blocks = blocks // 2
    mine = lax.axis_index("tp")
    place = lax.axis_index("dp")
    cube, core = mine // 2, mine % 2
    parity = place & 1
    scalars = jnp.stack([cube, core, cube_lengths[cube]]).astype(jnp.int32)

    def to_core(v):
        return lax.ppermute(v, "tp", pairs(tp, 1))

    def to_chip(v):
        return lax.ppermute(v, "tp", pairs(tp, 2))

    def to_place(v, mask):
        return lax.ppermute(v, "dp", pairs(dp, mask))

    bits = [1 << k for k in range(dp.bit_length() - 1)]

    def row(v):
        return v.reshape(1, -1)

    def wide(v):
        return jnp.pad(v, ((0, 0), (0, WIDE - group)))

    def projection(q, k, v):
        return jnp.concatenate([wide(q), wide(k), wide(v)], 1)

    qkv_own = jnp.concatenate([query_weight, key_weight, value_weight], 1)
    part = width // 2
    got = to_chip(lax.dynamic_slice(qkv_own, (parity * part, 0), (part, 3 * group)))
    other = to_place(got, 1)
    even = parity == 0
    qkv_far = jnp.where(even, jnp.concatenate([got, other], 0), jnp.concatenate([other, got], 0))
    small_own = jnp.concatenate([query_bias, value_bias, up_bias]).reshape(1, -1)
    small_far = to_chip(small_own)

    def bias_row(small):
        q, v = small[:, :group], small[:, group : 2 * group]
        return jnp.concatenate([wide(q), jnp.zeros_like(wide(q)), wide(v)], 1)

    out_far = to_chip(out_weight)
    out_side = to_core(jnp.concatenate([out_weight, out_far], 0))
    hidden_got = to_chip(jnp.where(even, up_weight, down_weight))
    hidden_other = to_place(hidden_got, 1)
    up_far = jnp.where(even, hidden_got, hidden_other)
    down_far = jnp.where(even, hidden_other, hidden_got)

    weight_0 = projection(query_weight, key_weight, value_weight)
    weight_1 = projection(qkv_far[:, :group], qkv_far[:, group : 2 * group], qkv_far[:, 2 * group :])

    full = (length, width)
    unit = 2 * length * width * width
    normed, qkv_0 = run(
        first_body, scalars, (blocks,),
        [cube_rows(width), whole((1, width)), whole((1, width)), whole((width, 3 * WIDE)), whole((1, 3 * WIDE))],
        [rows_of(width), rows_of(3 * WIDE)],
        [shape_of(full, BF16), shape_of((length, 3 * WIDE), BF16)],
        flops=unit, name="first_norm_project",
    )(tokens, row(first_gain), row(first_shift), weight_0, bias_row(small_own))

    def attend(qkv):
        step = length // 2
        return run(
            attend_body, scalars, (2,),
            [pl.BlockSpec((step, WIDE), lambda i, s: (i, 0)), whole((length, 3 * WIDE))],
            [pl.BlockSpec((step, WIDE), lambda i, s: (i, 0)), pl.BlockSpec((8, step), lambda i, s: (0, i))],
            [shape_of((length, WIDE), BF16), shape_of((8, length), F32)],
            flops=6 * unit, name="attend",
        )(qkv, qkv)

    att_0, log_0 = attend(qkv_0)
    (qkv_1,) = run(
        project_body, scalars, (blocks,),
        [rows_of(width), whole((width, 3 * WIDE)), whole((1, 3 * WIDE))],
        [rows_of(3 * WIDE)],
        [shape_of((length, 3 * WIDE), BF16)],
        flops=unit, name="project",
    )(normed, weight_1, bias_row(small_far))
    att_2 = to_core(att_0)
    att_1, log_1 = attend(qkv_1)
    att_3 = to_core(att_1)

    def tall(v):
        return jnp.pad(v, ((0, WIDE - group), (0, 0)))

    out_0, out_1 = tall(out_weight), tall(out_far)
    out_2, out_3 = tall(out_side[:group]), tall(out_side[group:])
    att_spec = rows_of(WIDE)
    out_spec = whole((WIDE, width))
    vector = whole((1, width))
    middle, normed_two = run(
        middle_body, scalars, (blocks,),
        [cube_rows(width)] + [att_spec] * 4 + [out_spec] * 4 + [vector] * 3,
        [rows_of(width)] * 2,
        [shape_of(full, F32), shape_of(full, BF16)],
        flops=unit, name="attention_out_norm",
    )(tokens, att_0, att_1, att_2, att_3, out_0, out_1, out_2, out_3, row(out_bias), row(second_gain), row(second_shift))

    def hidden_part(up, down, bias):
        return run(
            hidden_body, scalars, (blocks,),
            [rows_of(width), cube_rows(width), whole((width, hidden)), whole((hidden, width)), whole((1, hidden))],
            [rows_of(hidden), rows_of(hidden), rows_of(width), rows_of(width), whole((1, hidden))],
            [shape_of((length, hidden), BF16)] * 2 + [shape_of(full, BF16)] * 2 + [shape_of((1, hidden), F32)],
            flops=4 * unit, name="hidden_units",
        )(normed_two, cotangent, up, down, bias)

    def hidden_weights(active, upper):
        return run(
            hidden_weights_body, scalars, (hidden // WIDE,),
            [whole(full), pl.BlockSpec((length, WIDE), lambda i, s: (0, i)), pl.BlockSpec((length, WIDE), lambda i, s: (0, i)),
             pl.BlockSpec((1, length, width), lambda i, s: (s[0], 0, 0))],
            [pl.BlockSpec((width, WIDE), lambda i, s: (0, i)), pl.BlockSpec((WIDE, width), lambda i, s: (i, 0))],
            [shape_of((width, hidden), BF16), shape_of((hidden, width), BF16)],
            flops=2 * unit, name="hidden_weight_grads",
        )(normed_two, upper, active, cotangent)

    active_0, upper_0, feed_0, back_0, up_bias_0 = hidden_part(up_weight, down_weight, row(up_bias))
    side_back_0 = to_core(back_0)
    up_grad_0, down_grad_0 = hidden_weights(active_0, upper_0)
    active_1, upper_1, feed_1, back_1, up_bias_1 = hidden_part(up_far, down_far, small_far[:, 2 * group :])
    side_back_1 = to_core(back_1)
    up_grad_1, down_grad_1 = hidden_weights(active_1, upper_1)

    def own_half(v):
        return lax.dynamic_slice(v, (core * half, 0), (half, v.shape[1]))

    def side_half(v):
        return lax.dynamic_slice(v, ((1 - core) * half, 0), (half, v.shape[1]))

    side_feed = to_core((side_half(feed_0).astype(F32) + side_half(feed_1).astype(F32)).astype(BF16))
    own_output = (
        own_half(middle)
        + ((own_half(feed_0).astype(F32) + own_half(feed_1).astype(F32)) + side_feed.astype(F32))
        + row(down_bias).astype(F32)
    ).astype(BF16)

    def gather_rows(own):
        side = to_core(own)
        far = to_chip(own)
        far_side = to_core(far)
        result = jnp.zeros((tp, half, width), BF16)
        for where, block in ((mine, own), (mine ^ 1, side), (mine ^ 2, far), (mine ^ 3, far_side)):
            result = lax.dynamic_update_slice(result, block[None], (where, 0, 0))
        return result.reshape(slots, length, width)

    output = gather_rows(own_output)

    (
        grad_middle, grad_att_0, grad_att_1, inner_0, inner_1, out_grad_0, out_grad_1, sums_two,
    ) = run(
        back_two_body, scalars, (blocks,),
        [rows_of(width), cube_rows(width)] + [rows_of(width)] * 4 + [vector] + [out_spec] * 2 + [att_spec] * 2,
        [rows_of(width), att_spec, att_spec, pl.BlockSpec((8, ROWS), lambda i, s: (0, i)), pl.BlockSpec((8, ROWS), lambda i, s: (0, i)),
         out_spec, out_spec, whole((4, width))],
        [shape_of(full, F32), shape_of((length, WIDE), BF16), shape_of((length, WIDE), BF16), shape_of((8, length), F32), shape_of((8, length), F32),
         shape_of((WIDE, width), BF16), shape_of((WIDE, width), BF16), shape_of((4, width), F32)],
        scratch=[pltpu.VMEM((WIDE, width), F32)] * 2,
        flops=1.3 * unit, name="second_norm_back",
    )(middle, cotangent, back_0, back_1, side_back_0, side_back_1, row(second_gain), out_0, out_1, att_0, att_1)

    def attend_back(qkv, grad, logsum, inner):
        return run(
            attend_back_body, scalars, (1,),
            [whole((length, 3 * WIDE)), whole((length, WIDE)), whole((8, length)), whole((8, length))],
            [whole((length, 3 * WIDE))],
            [shape_of((length, 3 * WIDE), BF16)],
            flops=12 * unit, name="attend_back",
        )(qkv, grad, logsum, inner)[0]

    def qkv_weights(grads):
        return run(
            qkv_weights_body, scalars, (3,),
            [whole(full), pl.BlockSpec((length, WIDE), lambda i, s: (0, i))],
            [pl.BlockSpec((WIDE, width), lambda i, s: (i, 0)), pl.BlockSpec((1, WIDE), lambda i, s: (0, i))],
            [shape_of((3 * WIDE, width), BF16), shape_of((1, 3 * WIDE), F32)],
            flops=unit, name="project_weight_grads",
        )(normed, grads)

    def qkv_back(grads, weight, side):
        pick = lambda i, s: ((s[1] ^ side) * half_blocks + i, 0)
        return run(
            qkv_back_body, scalars, (half_blocks,),
            [pl.BlockSpec((ROWS, 3 * WIDE), pick), whole((width, 3 * WIDE))],
            [rows_of(width)],
            [shape_of((half, width), BF16)],
            flops=unit // 2, name="project_back",
        )(grads, weight)[0]

    grads_1 = attend_back(qkv_1, grad_att_1, log_1, inner_1)
    side_1 = to_core(qkv_back(grads_1, weight_1, 1))
    own_1 = qkv_back(grads_1, weight_1, 0)
    qkv_grad_1, qkv_bias_1 = qkv_weights(grads_1)
    grads_0 = attend_back(qkv_0, grad_att_0, log_0, inner_0)
    side_0 = to_core(qkv_back(grads_0, weight_0, 1))
    own_0 = qkv_back(grads_0, weight_0, 0)
    qkv_grad_0, qkv_bias_0 = qkv_weights(grads_0)

    token_spec = pl.BlockSpec((1, ROWS, width), lambda i, s: (s[0], s[1] * half_blocks + i, 0))
    own_grad, sums_one = run(
        back_one_body, scalars, (half_blocks,),
        [token_spec, own_rows(width, half_blocks)] + [rows_of(width)] * 4 + [vector],
        [rows_of(width), whole((2, width))],
        [shape_of((half, width), BF16), shape_of((2, width), F32)],
        name="first_norm_back",
    )(tokens, grad_middle, own_0, own_1, side_0, side_1, row(first_gain))
    input_grad = gather_rows(own_grad)

    def halve(v, mask):
        count = v.shape[0] // 2
        bit = (place // mask) & 1
        sent = to_place(lax.dynamic_slice(v, ((1 - bit) * count, 0), (count, v.shape[1])), mask)
        kept = lax.dynamic_slice(v, (bit * count, 0), (count, v.shape[1]))
        return (kept.astype(F32) + sent.astype(F32)).astype(BF16)

    def double(v, mask):
        bit = (place // mask) & 1
        other = to_place(v, mask)
        return jnp.where(bit == 0, jnp.concatenate([v, other], 0), jnp.concatenate([other, v], 0))

    def over_cubes(near, far):
        total = (near.astype(F32) + to_chip(far).astype(F32)).astype(BF16)
        for mask in bits:
            total = halve(total, mask)
        for mask in reversed(bits):
            total = double(total, mask)
        return total

    def strip(v):
        return jnp.concatenate([v[k * WIDE : k * WIDE + group] for k in range(v.shape[0] // WIDE)], 0)

    hidden_grad = over_cubes(
        jnp.concatenate([up_grad_0, down_grad_0], 0), jnp.concatenate([up_grad_1, down_grad_1], 0)
    )
    mixed_grad = over_cubes(
        jnp.concatenate([strip(out_grad_0), strip(qkv_grad_0)], 0),
        jnp.concatenate([strip(out_grad_1), strip(qkv_grad_1)], 0),
    )

    def vectors_over_cubes(near, far):
        total = near + to_chip(far)
        for mask in bits:
            total = total + to_place(total, mask)
        return total

    early = vectors_over_cubes(
        jnp.concatenate([sums_two, up_bias_0], 0), jnp.concatenate([sums_two, up_bias_1], 0)
    )
    first_sums = sums_one + to_core(sums_one)
    late = vectors_over_cubes(
        jnp.concatenate([first_sums, qkv_bias_0], 0), jnp.concatenate([first_sums, qkv_bias_1], 0)
    )
    mixed_grad = mixed_grad.astype(F32)
    hidden_grad = hidden_grad.astype(F32)

    def turned(k):
        return mixed_grad[k * group : (k + 1) * group].T

    return (
        output,
        input_grad,
        turned(1),
        late[2, :group],
        turned(2),
        turned(3),
        late[2, 2 * WIDE : 2 * WIDE + group],
        mixed_grad[:group],
        early[2],
        late[0],
        late[1],
        early[0],
        early[1],
        hidden_grad[:width],
        early[4],
        hidden_grad[width:],
        early[3],
    )


def solution(mesh):
    dp, tp = mesh.shape["dp"], mesh.shape["tp"]
    placed = (
        P("dp", None, None),
        P("dp"),
        P(None, "tp"),
        P("tp"),
        P(None, "tp"),
        P(None, "tp"),
        P("tp"),
        P("tp", None),
        P(),
        P(),
        P(),
        P(),
        P(),
        P(None, "tp"),
        P("tp"),
        P("tp", None),
        P(),
        P("dp", None, None),
    )
    return jax.shard_map(
        partial(local, dp, tp),
        mesh=mesh,
        in_specs=placed,
        out_specs=(
            P("dp", None, None),
            P("dp", None, None),
            P(None, "tp"),
            P("tp"),
            P(None, "tp"),
            P(None, "tp"),
            P("tp"),
            P("tp", None),
            P(),
            P(),
            P(),
            P(),
            P(),
            P(None, "tp"),
            P("tp"),
            P("tp", None),
            P(),
        ),
        check_vma=False,
    )
```

```python
from functools import partial

import jax
import jax.numpy as jnp
from jax import lax
from jax.experimental import pallas as pl
from jax.experimental.pallas import tpu as pltpu
from jax.sharding import PartitionSpec as P

HEAD_DIM = 64
SHORT = 864
ROWS = 512
BLOCK = 256
LANES = 128
WIDE = 256
EPS = 1e-06
LOG2E = 1.4426950408889634
LN2 = 0.6931471805599453
BF16 = jnp.bfloat16
F32 = jnp.float32

NN = (((1,), (0,)), ((), ()))
NT = (((1,), (1,)), ((), ()))
TN = (((0,), (0,)), ((), ()))


def dot(left, right, dims):
    return lax.dot_general(left, right, dims, preferred_element_type=F32)


def shape_of(shape, dtype):
    return jax.ShapeDtypeStruct(shape, dtype)


def run(body, scalars, grid, in_specs, out_specs, out_shape, scratch=(), alias=None, name=None, room=20):
    def call(*arrays):
        return pl.pallas_call(
            body,
            grid_spec=pltpu.PrefetchScalarGridSpec(
                num_scalar_prefetch=2,
                grid=grid,
                in_specs=in_specs,
                out_specs=out_specs,
                scratch_shapes=list(scratch),
            ),
            out_shape=out_shape,
            input_output_aliases={k + 2: v for k, v in (alias or {}).items()},
            compiler_params=pltpu.CompilerParams(vmem_limit_bytes=room << 20),
            cost_estimate=pl.CostEstimate(flops=1000, transcendentals=0, bytes_accessed=1000),
            name=name,
        )(*scalars, *arrays)

    return call


def in_hbm(v):
    return pltpu.with_memory_space_constraint(v, pltpu.HBM)


def whole(shape):
    return pl.BlockSpec(shape, lambda i, s, n: (0,) * len(shape))


def rows_of(width, at=0):
    return pl.BlockSpec((ROWS, width), lambda i, s, n: (i, at))


def cube_rows(width):
    return pl.BlockSpec((1, ROWS, width), lambda i, s, n: (s[0], i, 0))


def normalize(values):
    center = values - jnp.mean(values, -1, keepdims=True)
    inverse = lax.rsqrt(jnp.mean(center * center, -1, keepdims=True) + EPS)
    return center * inverse, inverse


def norm_back(grad, normal, inverse, gain):
    scaled = grad * gain
    return inverse * (
        scaled
        - jnp.mean(scaled, -1, keepdims=True)
        - normal * jnp.mean(scaled * normal, -1, keepdims=True)
    )


def column_sums(values):
    return jnp.sum(values, 0, keepdims=True)


def sum_rows(values):
    return dot(jnp.ones((8, values.shape[0]), BF16), values, NN)[0:1]


def accumulate(ref, value):
    first = pl.program_id(0) == 0

    @pl.when(first)
    def _():
        ref[...] = value

    @pl.when(jnp.logical_not(first))
    def _():
        ref[...] += value


SCALE = HEAD_DIM**-0.5 * LOG2E


def scaled(part):
    lane = lax.broadcasted_iota(jnp.int32, (1, part.shape[1]), 1)
    return (part * jnp.where(lane < LANES, SCALE, 1.0)).astype(BF16)


def pack_body(s, n, query, key, value, out, g1, s1, g2, s2, ob, db, ub, qb, vb, sent, third, params, sems):
    extra = query.shape[0] - LANES
    copies = []

    def move(source, target):
        copies.append(pltpu.make_async_copy(source, target, sems.at[len(copies)]))
        copies[-1].start()

    for k, weight in enumerate((query, key, value)):
        last = weight.at[pl.ds(LANES, extra)]
        move(weight.at[pl.ds(0, LANES)], sent.at[pl.ds(k * LANES, LANES)])
        move(last, sent.at[pl.ds(3 * LANES + k * extra, extra)])
        move(last, third.at[pl.ds(k * LANES, extra)])
    top = 3 * LANES + 3 * extra + out.shape[0]
    move(out, sent.at[pl.ds(top - out.shape[0], out.shape[0])])
    for k in range(3):
        third[k * LANES + extra : (k + 1) * LANES] = jnp.zeros((LANES - extra, third.shape[1]), BF16)
    table = [v[...].astype(F32).reshape(1, -1) for v in (g1, s1, g2, s2, ob, db, ub)]
    query_bias, value_bias = (v[...].astype(F32).reshape(1, -1) for v in (qb, vb))
    hole = jnp.zeros((1, LANES), F32)
    gap = jnp.zeros((1, LANES - extra), F32)
    ends = [jnp.concatenate([v[:, LANES:], gap], 1) for v in (query_bias, value_bias)]
    table.append(jnp.concatenate([query_bias[:, :LANES], hole, value_bias[:, :LANES], ends[0], hole, ends[1]], 1))
    table = jnp.concatenate(table, 0)
    params[...] = table
    sent[top:] = jnp.concatenate([table, table], 0).astype(BF16)
    for copy in copies:
        copy.wait()


def first_body(s, n, tokens, params, pair_weight, third_weight, normed_out, pair_out, third_out):
    normal, _ = normalize(tokens[0].astype(F32))
    normed = (normal * params[0:1] + params[1:2]).astype(BF16)
    normed_out[...] = normed
    span = pair_weight.shape[0]
    pair_out[...] = scaled(dot(normed, pair_weight[...], NT) + params[7:8, :span])
    third_out[...] = scaled(dot(normed, third_weight[...], NT) + params[7:8, span:])


def head_view(ref, rows, start, head, heads):
    value = ref[rows, start : start + LANES]
    if heads == 1:
        return value
    lane = lax.broadcasted_iota(jnp.int32, (1, LANES), 1)
    keep = (lane < HEAD_DIM) if head == 0 else (lane >= HEAD_DIM)
    return jnp.where(keep, value, jnp.zeros((), BF16))


def pick_head(values):
    if len(values) == 1:
        return values[0]
    lane = lax.broadcasted_iota(jnp.int32, (1, LANES), 1)
    return jnp.where(lane < HEAD_DIM, values[0], values[1])


def attend_part(queries, sources, attended, logsum, limit, block):
    count = queries[0].shape[0] // block
    keys = [source[:limit, LANES : 2 * LANES] for source in sources]
    values = [source[:limit, 2 * LANES :] for source in sources]

    def scores(unit):
        at, head = unit
        rows = slice(at * block, (at + 1) * block)
        return dot(head_view(queries[head // 2], rows, 0, head, 2 - head // 2), keys[head // 2], NT)

    units = [(at, head) for at in range(count) for head in range(3)]
    current = scores(units[0])
    done = []
    for index, (at, head) in enumerate(units):
        following = scores(units[index + 1]) if index + 1 < len(units) else None
        peak = jnp.max(current, -1, keepdims=True)
        expo = jnp.exp2(current - peak)
        total = jnp.sum(expo, -1, keepdims=True)
        mixed = dot(expo.astype(BF16), values[head // 2], NN)
        done.append((mixed * (1.0 / total), jnp.broadcast_to(peak + jnp.log2(total), mixed.shape)))
        current = following
        if head == 2:
            rows = slice(at * block, (at + 1) * block)
            attended[rows, :LANES] = pick_head([done[0][0], done[1][0]]).astype(BF16)
            attended[rows, LANES:] = done[2][0].astype(BF16)
            table = jnp.transpose(pick_head([done[0][1], done[1][1]]))
            logsum[:8, rows] = jnp.concatenate([table[0:4], table[HEAD_DIM : HEAD_DIM + 4]], 0)
            logsum[8:, rows] = jnp.transpose(done[2][1])[:8]
            done = []


def attend_body(s, n, query_pair, query_third, pair, third, attended, logsum):
    full = pair.shape[0]

    @pl.when(n[s[0]] == full)
    def _():
        attend_part((query_pair, query_third), (pair, third), attended, logsum, full, BLOCK)

    @pl.when(n[s[0]] != full)
    def _():
        attend_part((query_pair, query_third), (pair, third), attended, logsum, SHORT, BLOCK)


def attend_back_part(qkv, grad, logsum, inner, grads, heads, limit, block, full):
    count = -(-limit // block)
    keys = qkv[:limit, LANES : 2 * LANES]
    values = qkv[:limit, 2 * LANES :]

    def span(at):
        return slice(at * block, min((at + 1) * block, limit))

    def front(unit):
        head, at = unit
        query = head_view(qkv, span(at), 0, head, heads)
        pull = head_view(grad, span(at), 0, head, heads)
        return dot(keys, query, NT), dot(values, pull, NT), query, pull

    def put(rows, start, head, value):
        value = value.astype(BF16)
        if head == 1:
            value = pick_head([grads[rows, start : start + LANES], value])
        grads[rows, start : start + LANES] = value

    units = [(head, at) for head in range(heads) for at in range(count)]
    current = front(units[0])
    for index, (head, at) in enumerate(units):
        following = front(units[index + 1]) if index + 1 < len(units) else None
        scores, grad_probs, query, pull = current
        at_row = slice(4 * head, 4 * head + 1)
        probs = jnp.exp2(scores - logsum[at_row, span(at)])
        grad_scores = (probs * (grad_probs - inner[at_row, span(at)])).astype(BF16)
        value_part = dot(probs.astype(BF16), pull, NN)
        key_part = dot(grad_scores, query, NN)
        grad_values = value_part if at == 0 else grad_values + value_part
        grad_keys = key_part if at == 0 else grad_keys + key_part
        put(span(at), 0, head, dot(grad_scores, keys, TN) * HEAD_DIM**-0.5)
        if at == count - 1:
            put(slice(0, limit), LANES, head, grad_keys * LN2)
            put(slice(0, limit), 2 * LANES, head, grad_values)
        current = following
    if limit < full:
        grads[limit:, :] = jnp.zeros((full - limit, grads.shape[1]), BF16)


def attend_back_body(heads, s, n, qkv, grad, logsum, inner, grads):
    full = qkv.shape[0]

    @pl.when(n[s[0]] == full)
    def _():
        attend_back_part(qkv, grad, logsum, inner, grads, heads, full, BLOCK, full)

    @pl.when(n[s[0]] != full)
    def _():
        attend_back_part(qkv, grad, logsum, inner, grads, heads, SHORT, BLOCK, full)


def middle_body(s, n, tokens, params, *refs):
    arrays, weights, (middle_out, normed_out) = refs[:4], refs[4:8], refs[8:]
    branch = params[4:5]
    for array, weight in zip(arrays, weights):
        branch = branch + dot(array[:, : weight.shape[0]], weight[...], NN)
    middle = tokens[0].astype(F32) + branch
    middle_out[...] = middle.astype(BF16)
    normal, _ = normalize(middle)
    normed_out[...] = (normal * params[2:3] + params[3:4]).astype(BF16)


def gelu_and_slope(values):
    t = 1.0 / (1.0 + (0.3275911 * 0.7071067811865476) * jnp.abs(values))
    series = t * (
        (0.5 * 0.254829592)
        + t * ((0.5 * -0.284496736) + t * ((0.5 * 1.421413741) + t * ((0.5 * -1.453152027) + t * (0.5 * 1.061405429))))
    )
    decay = jnp.exp2(values * values * (-0.5 * LOG2E))
    tail = series * decay
    share = jnp.where(values >= 0, 1.0 - tail, tail)
    return values * share, share + values * (decay * 0.3989422804014327)


def hidden_part(normed, grad_feed, up, down, bias, active_out, upper_out, bias_out, put):
    count = normed.shape[0] // BLOCK

    def front(at):
        rows = slice(at * BLOCK, (at + 1) * BLOCK)
        return dot(normed[rows], up[...], NN), dot(grad_feed[rows], down[...], NT)

    current = front(0)
    total = None
    for at in range(count):
        following = front(at + 1) if at + 1 < count else None
        rows = slice(at * BLOCK, (at + 1) * BLOCK)
        active, slope = gelu_and_slope(current[0] + bias)
        active = active.astype(BF16)
        active_out[rows] = active
        grad_upper = (current[1] * slope).astype(BF16)
        upper_out[rows] = grad_upper
        put(rows, dot(active, down[...], NN), dot(grad_upper, up[...], NT))
        sums = sum_rows(grad_upper)
        total = sums if total is None else total + sums
        current = following
    accumulate(bias_out, total)


def hidden_own_body(s, n, normed, cot, up, down, params, feed_grad_out, active_out, upper_out, feed_out, back_out, bias_out):
    position = pl.program_id(0) * ROWS + lax.broadcasted_iota(jnp.int32, (ROWS, 1), 0)
    grad_feed = jnp.where(position < n[s[0]], cot[0], jnp.zeros((), BF16))
    feed_grad_out[...] = grad_feed

    def put(rows, feed, back):
        feed_out[rows] = feed.astype(BF16)
        back_out[rows] = back.astype(BF16)

    hidden_part(normed[...], grad_feed, up, down, params[6:7], active_out, upper_out, bias_out, put)


def hidden_far_body(s, n, normed, grad_feed, feed_in, back_in, g0, g1, o0, o1, small, *refs):
    (active_out, upper_out, feed_out, back_out, bias_out), (up, down, sems) = refs[:5], refs[5:]
    part = g0.shape[0]

    @pl.when(pl.program_id(0) == 0)
    def _():
        def fill(first, second):
            copies = []
            for at, (target, sources) in enumerate(((up, first), (down, second))):
                rows = (pl.ds(0, part), pl.ds(part, target.shape[0] - part))
                for k, source in enumerate(sources):
                    copies.append(pltpu.make_async_copy(source, target.at[rows[k]], sems.at[2 * at + k]))
            for copy in copies:
                copy.start()
            for copy in copies:
                copy.wait()

        @pl.when(s[2] == 0)
        def _():
            fill((g0, g1), (o0, o1))

        @pl.when(s[2] != 0)
        def _():
            fill((o0, o1), (g0, g1))

    def put(rows, feed, back):
        feed_out[rows] = (feed_in[rows].astype(F32) + feed).astype(BF16)
        back_out[rows] = (back_in[rows].astype(F32) + back).astype(BF16)

    hidden_part(normed[...], grad_feed[...], up, down, small[6:7].astype(F32), active_out, upper_out, bias_out, put)


def output_body(s, n, middle, feed, side, params, own_out, all_out):
    total = feed[...].astype(F32) + side[...].astype(F32)
    own = (middle[...].astype(F32) + total + params[5:6]).astype(BF16)
    own_out[...] = own
    all_out[0] = own


def back_two_body(s, n, middle, grad_feed, g0, g1, params, w0, w1, a0, a1, branch_out, *refs):
    grad_tiles, inner_outs, sums_out = refs[:4], refs[4:8], refs[8]
    normal, inverse = normalize(middle[...].astype(F32))
    grad_normed = g0[...].astype(F32) + g1[...].astype(F32)
    grad_output = grad_feed[...].astype(F32)
    grad_middle = grad_output + norm_back(grad_normed, normal, inverse, params[2:3])
    grad_branch = grad_middle.astype(BF16)
    branch_out[...] = grad_branch
    sums = jnp.concatenate(
        [
            column_sums(grad_normed * normal),
            column_sums(grad_normed),
            column_sums(grad_branch.astype(F32)),
            column_sums(grad_output),
        ],
        0,
    )
    accumulate(sums_out, sums)
    lane = lax.broadcasted_iota(jnp.int32, (8, LANES), 1)
    head = lax.broadcasted_iota(jnp.int32, (8, LANES), 0)
    member = (lane // HEAD_DIM == head // 4).astype(BF16)
    for k, (weight, array) in enumerate(((w0, a0), (w1, a1))):
        grad_att = dot(grad_branch, weight[...], NT).astype(BF16)
        extra = grad_att.shape[1] - LANES
        gap = jnp.zeros((grad_att.shape[0], LANES - extra), BF16)
        for t in range(2):
            lanes = slice(t * LANES, (t + 1) * LANES)
            part = grad_att[:, :LANES] if t == 0 else jnp.concatenate([grad_att[:, LANES:], gap], 1)
            grad_tiles[2 * k + t][...] = part
            product = part.astype(F32) * array[:, lanes].astype(F32)
            high = product.astype(BF16)
            low = (product - high.astype(F32)).astype(BF16)
            inner_outs[2 * k + t][...] = dot(member, high, NT) + dot(member, low, NT)


def back_one_body(s, n, tokens, grad_middle, g0, g1, g2, g3, params, own_out, all_out, sums_out):
    normal, inverse = normalize(tokens[0].astype(F32))
    grad_normed = (g0[...].astype(F32) + g1[...].astype(F32)) + (g2[...].astype(F32) + g3[...].astype(F32))
    accumulate(
        sums_out, jnp.concatenate([column_sums(grad_normed * normal), column_sums(grad_normed)], 0)
    )
    back = norm_back(grad_normed, normal, inverse, params[0:1])
    own = (grad_middle[...].astype(F32) + back).astype(BF16)
    own_out[...] = own
    all_out[0] = own


def pairs(count, mask):
    return [(i, i ^ mask) for i in range(count)]


def overlap(moves, kernel=None, inputs=()):
    operands, inputs = lax.optimization_barrier((tuple(v for _, v in moves), tuple(inputs)))
    received = tuple(move(v) for (move, _), v in zip(moves, operands))
    results = tuple(kernel(*inputs)) if kernel else ()
    return lax.optimization_barrier((received, results))


def after(value, *others):
    return lax.optimization_barrier((value, *others))[0]


def local(
    dp, tp,
    tokens, cube_lengths, query_weight, query_bias, key_weight, value_weight, value_bias,
    out_weight, out_bias, first_gain, first_shift, second_gain, second_shift,
    up_weight, up_bias, down_weight, down_bias, cotangent,
):
    slots, length, width = tokens.shape
    group = query_weight.shape[1]
    hidden = up_weight.shape[1]
    blocks = length // ROWS
    half = length // 2
    half_rows = half // 2
    mine = lax.axis_index("tp")
    place = lax.axis_index("dp")
    cube, core = mine // 2, mine % 2
    parity = place & 1
    scalars = (jnp.stack([cube, core, parity, mine]).astype(jnp.int32), cube_lengths)
    bits = [1 << k for k in range(dp.bit_length() - 1)]

    def to_core(v):
        return lax.ppermute(v, "tp", pairs(tp, 1))

    def to_chip(v):
        return lax.ppermute(v, "tp", pairs(tp, 2))

    def to_place(v, mask):
        return lax.ppermute(v, "dp", pairs(dp, mask))

    full = (length, width)
    span = 3 * LANES
    extra = group - LANES
    vectors = whole((8, width))
    part_spec = whole((span, width))
    part_shape = shape_of((length, span), BF16)

    top = span + 3 * extra + group
    far_shape = (top + 16, width)
    anywhere = pl.BlockSpec(memory_space=pl.ANY)
    vector = pl.BlockSpec((width,), lambda i, s, n: (0,))
    short_vector = pl.BlockSpec((group,), lambda i, s, n: (0,))
    sent, third_0, params = run(
        pack_body, scalars, (1,),
        [anywhere] * 4 + [vector] * 7 + [short_vector] * 2,
        [whole(far_shape), part_spec, vectors],
        [shape_of(far_shape, BF16), shape_of((span, width), BF16), shape_of((8, width), F32)],
        scratch=[pltpu.SemaphoreType.DMA((10,))],
        name="pack_weights", room=10,
    )(
        *map(in_hbm, (
            query_weight.T, key_weight.T, value_weight.T, out_weight, first_gain, first_shift, second_gain, second_shift,
            out_bias, down_bias, up_bias, query_bias, value_bias,
        ))
    )
    far = to_chip(sent)

    def spread(rows):
        gap = ((0, 0), (0, LANES - extra), (0, 0))
        return jnp.pad(rows.reshape(3, extra, width), gap).reshape(span, width)

    normed, part_0, part_1 = run(
        first_body, scalars, (blocks,),
        [cube_rows(width), vectors, part_spec, part_spec],
        [rows_of(width), rows_of(span), rows_of(span)],
        [shape_of(full, BF16), part_shape, part_shape],
        name="first_norm_project", room=10,
    )(in_hbm(tokens), params, sent, third_0)
    pair_0 = sent[:span]

    def attend(pair, third):
        step = length // 2
        query = pl.BlockSpec((step, LANES), lambda i, s, n: (i, 0))
        return run(
            attend_body, scalars, (2,),
            [query, query, whole((length, span)), whole((length, span))],
            [pl.BlockSpec((step, 2 * LANES), lambda i, s, n: (i, 0)), pl.BlockSpec((16, step), lambda i, s, n: (0, i))],
            [shape_of((length, 2 * LANES), BF16), shape_of((16, length), F32)],
            name="attend", room=14,
        )(pair, third, pair, third)

    def project(weight, bias, at):
        return scaled(dot(normed, weight, NT) + bias[:, at * span : (at + 1) * span])

    first_rows = (2 * hidden // 3) // LANES * LANES
    hidden_sent = jnp.where(parity == 0, up_weight, down_weight)
    att_0, log_0 = attend(after(part_0, hidden_sent), part_1)
    far = after(far, att_0)
    pair_1, third_1 = far[:span], spread(far[span : span + 3 * extra])
    bias_1 = far[top + 7 : top + 8].astype(F32)
    part_2 = project(pair_1, bias_1, 0)
    part_3 = project(third_1, bias_1, 1)
    out_sent = jnp.concatenate([out_weight, far[span + 3 * extra : top]], 0)
    got_0 = to_chip(after(hidden_sent[:first_rows], far))
    got_1 = to_chip(after(hidden_sent[first_rows:], far))
    (side_0, out_side), (att_1, log_1) = overlap([(to_core, att_0), (to_core, out_sent)], attend, (part_2, part_3))
    side_1 = to_core(att_1)
    other_0 = to_place(after(got_0, att_1), 1)

    double_tile = rows_of(2 * LANES)

    def out_block(at):
        return pl.BlockSpec((group, width), lambda i, s, n: (at, 0))

    out_specs = [out_block(0), out_block((span + 3 * extra) // group), out_block(0), out_block(1)]
    middle, normed_two = run(
        middle_body, scalars, (blocks,),
        [cube_rows(width), vectors] + [double_tile] * 4 + out_specs,
        [rows_of(width)] * 2,
        [shape_of(full, BF16), shape_of(full, BF16)],
        name="attention_out_norm", room=12,
    )(in_hbm(tokens), params, att_0, att_1, side_0, side_1, out_weight, far, out_side, out_side)

    own_spec = pl.BlockSpec((half_rows, width), lambda i, s, n: (s[1] * 2 + i, 0))
    plain = pl.BlockSpec((half_rows, width), lambda i, s, n: (i, 0))
    own_out_specs = [plain, pl.BlockSpec((1, half_rows, width), lambda i, s, n: (s[3], i, 0))]
    own_shapes = [shape_of((half, width), BF16), shape_of((tp, half, width), BF16)]

    def side_half(v):
        return lax.dynamic_slice(v, ((1 - core) * half, 0), (half, v.shape[1]))

    def place_block(result, block, where, at):
        return lax.dynamic_update_slice(result, block[None], (where, at, 0))

    def bit_of(mask):
        return (place // mask) & 1

    def half_at(v, bit):
        count = v.shape[-2] // 2
        return lax.dynamic_slice_in_dim(v, bit * count, count, v.ndim - 2)

    def half_out(v, mask):
        return half_at(v, 1 - bit_of(mask))

    def half_kept(v, mask):
        return half_at(v, bit_of(mask))

    def add(a, b):
        return (a.astype(F32) + b.astype(F32)).astype(BF16)

    def join(v, other, mask):
        return jnp.where(bit_of(mask) == 0, jnp.concatenate([v, other], 0), jnp.concatenate([other, v], 0))

    both = shape_of((length, hidden), BF16)
    hidden_shapes = [both, both, shape_of(full, BF16), shape_of(full, BF16), shape_of((1, hidden), F32)]

    hidden_specs = [rows_of(hidden), rows_of(hidden), rows_of(width), rows_of(width), whole((1, hidden))]

    own_call = run(
        hidden_own_body, scalars, (blocks,),
        [rows_of(width), cube_rows(width), whole((width, hidden)), whole((hidden, width)), vectors],
        [rows_of(width)] + hidden_specs,
        [shape_of(full, BF16)] + hidden_shapes,
        name="hidden_own", room=19,
    )
    grad_feed, active_0, upper_0, feed, back, up_bias_0 = own_call(normed_two, in_hbm(cotangent), in_hbm(up_weight), in_hbm(down_weight), params)
    other_1 = to_place(after(got_1, up_bias_0), 1)

    def hidden_grads(active, upper):
        return dot(normed_two, upper, TN).astype(BF16), dot(active, grad_feed, TN).astype(BF16)

    near = hidden_grads(active_0, upper_0)
    orders = [bits, bits[1:2] + bits[:1] + bits[2:]]
    far_call = run(
        hidden_far_body, scalars, (blocks,),
        [rows_of(width)] * 4 + [anywhere] * 4 + [pl.BlockSpec((16, width), lambda i, s, n: (top // 16, 0))],
        hidden_specs,
        hidden_shapes,
        scratch=[pltpu.VMEM((width, hidden), BF16), pltpu.VMEM((hidden, width), BF16), pltpu.SemaphoreType.DMA((4,))],
        name="hidden_far", room=20,
    )

    sent_near = [half_out(v, order[0]) for v, order in zip(near, orders)]

    def over(order, k):
        return lambda v: to_place(v, order[k])

    got_near, (active_1, upper_1, feed, back, up_bias_1) = overlap(
        [(over(order, 0), v) for v, order in zip(sent_near, orders)],
        far_call,
        (normed_two, grad_feed, feed, back, got_0, got_1, other_0, other_1, far),
    )
    side_back = to_core(back)
    side_feed = to_core(side_half(feed))
    away = hidden_grads(active_1, upper_1)
    own_output, output = run(
        output_body, scalars, (2,),
        [own_spec] * 2 + [plain, vectors],
        own_out_specs, own_shapes, name="output", room=8,
    )(after(middle, *away), feed, side_feed, params)
    sent_away = [half_out(v, order[0]) for v, order in zip(away, orders)]

    tile = rows_of(LANES)
    tile_shape = shape_of((length, LANES), BF16)
    inner_shape = shape_of((8, length), F32)
    two_call = run(
        back_two_body, scalars, (blocks,),
        [rows_of(width)] * 4 + [vectors] + out_specs[:2] + [double_tile] * 2,
        [rows_of(width)] + [tile] * 4 + [pl.BlockSpec((8, ROWS), lambda i, s, n: (0, i))] * 4 + [whole((4, width))],
        [shape_of(full, BF16)] + [tile_shape] * 4 + [inner_shape] * 4 + [shape_of((4, width), F32)],
        name="second_norm_back", room=16,
    )
    (far_output_0, side_output, *got_away), results = overlap(
        [(to_chip, own_output[:half_rows]), (to_core, own_output)] + [(over(order, 0), v) for v, order in zip(sent_away, orders)],
        two_call,
        (middle, grad_feed, back, side_back, params, out_weight, far, att_0, att_1),
    )
    grad_branch, gt_0, gt_1, gt_2, gt_3, in_0, in_1, in_2, in_3, sums_two = results

    def attend_back(qkv, grad, logsum, inner, count):
        at = 2 - count
        return run(
            partial(attend_back_body, count), scalars, (1,),
            [whole((length, span)), whole((length, LANES)), pl.BlockSpec((8, length), lambda i, s, n: (at, 0)), whole((8, length))],
            [whole((length, span))],
            [part_shape],
            name="attend_back", room=13,
        )(qkv, grad, logsum, inner)

    def weight_grad(grads):
        return dot(grads, normed, TN).astype(BF16)

    def third_only(v):
        return v.reshape(3, LANES, width)[:, :extra].reshape(3 * extra, width)

    pair_back, third_back = partial(attend_back, count=2), partial(attend_back, count=1)
    (far_output_1, across_output_0), (grads_2,) = overlap(
        [(to_chip, own_output[half_rows:]), (to_core, far_output_0)], pair_back, (part_2, gt_2, log_1, in_2)
    )
    out_grads = [dot(a, grad_branch, TN).astype(BF16)[:group] for a in (att_0, att_1)]
    stage_2 = [
        jnp.stack([add(half_kept(v, order[0]), g), add(half_kept(w, order[0]), h)])
        for v, g, w, h, order in zip(near, got_near, away, got_away, orders)
    ]
    sent_2 = [half_out(v, order[1]) for v, order in zip(stage_2, orders)]
    pair_away = weight_grad(grads_2)
    (across_output_1, pair_far, *got_second), (grads_0,) = overlap(
        [(to_core, far_output_1), (to_chip, pair_away)] + [(over(order, 1), v) for v, order in zip(sent_2, orders)],
        pair_back,
        (part_0, gt_0, log_0, in_0),
    )
    for where, at, block in (
        (1, 0, side_output), (2, 0, far_output_0), (2, half_rows, far_output_1), (3, 0, across_output_0), (3, half_rows, across_output_1)
    ):
        output = place_block(output, block, mine ^ where, at)
    output = output.reshape(slots, length, width)

    stage_3 = [add(half_kept(v, order[1]), g) for v, g, order in zip(stage_2, got_second, orders)]
    pair = add(weight_grad(grads_0), pair_far)
    sent_pair = half_out(pair, bits[0])
    back_most = dot(grads_2, pair_1, NN) + dot(grads_0, pair_0, NN)
    (got_pair, *got_third), (grads_3,) = overlap(
        [(over(bits, 0), sent_pair)] + [(to_chip, v[1]) for v in stage_3], third_back, (part_3, gt_3, log_1, in_3)
    )
    third_away = third_only(weight_grad(grads_3))
    back_most = (back_most + dot(grads_3, third_1, NN)).astype(BF16)
    side_most_sent = side_half(back_most)
    stage_4 = [add(v[0], g) for v, g in zip(stage_3, got_third)]
    pair = add(half_kept(pair, bits[0]), got_pair)
    sent_pair = half_out(pair, bits[1])
    last_away = jnp.concatenate([out_grads[1], third_away], 0)
    (got_pair, last_far, side_most, *got_fourth), (grads_1,) = overlap(
        [(over(bits, 1), sent_pair), (to_chip, last_away), (to_core, side_most_sent)] + [(over(bits, 2), v) for v in stage_4],
        third_back,
        (part_1, gt_1, log_0, in_1),
    )
    back_last = dot(grads_1, third_0, NN).astype(BF16)
    last = add(jnp.concatenate([out_grads[0], third_only(weight_grad(grads_1))], 0), last_far)
    side_last_sent = side_half(back_last)
    sent_last = half_out(last, bits[0])
    pair = add(half_kept(pair, bits[1]), got_pair)
    side_last = to_core(side_last_sent)

    token_spec = pl.BlockSpec((1, half_rows, width), lambda i, s, n: (s[0], s[1] * 2 + i, 0))
    own_grad, input_grad, sums_one = run(
        back_one_body, scalars, (2,),
        [token_spec, own_spec, own_spec, own_spec, plain, plain, vectors],
        own_out_specs + [whole((2, width))],
        own_shapes + [shape_of((2, width), F32)],
        name="first_norm_back", room=14,
    )(in_hbm(tokens), grad_branch, back_most, back_last, side_most, side_last, params)

    third_rows = half // 3
    totals = [add(v, g) for v, g in zip(stage_4, got_fourth)]
    (far_0, side_grad, first_sums, got_pair, got_last), _ = overlap(
        [(to_chip, own_grad[:third_rows]), (to_core, own_grad), (to_core, sums_one), (over(bits, 2), pair), (over(bits, 0), sent_last)]
    )
    pair = add(pair, got_pair)
    last = add(half_kept(last, bits[0]), got_last)
    for mask in bits[3:]:
        pair, last = (add(v, to_place(v, mask)) for v in (pair, last))
        totals = [add(v, to_place(v, mask)) for v in totals]
    first_sums = sums_one + first_sums
    def bias_sums(pair, third):
        return jnp.concatenate([sum_rows(pair), sum_rows(third)], 1)

    shared = [sums_two, first_sums]
    sums = jnp.concatenate(shared + [up_bias_0, bias_sums(grads_0, grads_1)], 0)
    sums_away = jnp.concatenate(shared + [up_bias_1, bias_sums(grads_2, grads_3)], 0)
    (far_1, across_0, got_sums, got_pair, got_last, *got_totals), _ = overlap(
        [(to_chip, own_grad[third_rows : 2 * third_rows]), (to_core, far_0), (to_chip, sums_away), (over(bits, 1), pair), (over(bits, 1), last)]
        + [(over(order, 1), v) for v, order in zip(totals, orders)]
    )
    totals = [join(v, g, order[1]) for v, g, order in zip(totals, got_totals, orders)]
    pair = join(pair, got_pair, bits[1])
    last = add(last, got_last)
    sums = sums + got_sums
    (far_2, across_1, got_sums, got_pair, got_last, *got_totals), _ = overlap(
        [(to_chip, own_grad[2 * third_rows :]), (to_core, far_1), (over(bits, 0), sums), (over(bits, 0), pair), (over(bits, 2), last)]
        + [(over(order, 0), v) for v, order in zip(totals, orders)]
    )
    totals = [join(v, g, order[0]).astype(F32) for v, g, order in zip(totals, got_totals, orders)]
    pair = join(pair, got_pair, bits[0]).astype(F32)
    last = add(last, got_last)
    sums = sums + got_sums
    (across_2, got_sums, got_last), _ = overlap([(to_core, far_2), (over(bits, 1), sums), (over(bits, 0), last)])
    last = join(last, got_last, bits[0]).astype(F32)
    sums = sums + got_sums
    for mask in bits[2:]:
        sums = sums + to_place(sums, mask)
    for where, at, block in (
        (1, 0, side_grad), (2, 0, far_0), (2, third_rows, far_1), (2, 2 * third_rows, far_2),
        (3, 0, across_0), (3, third_rows, across_1), (3, 2 * third_rows, across_2),
    ):
        input_grad = place_block(input_grad, block, mine ^ where, at)
    input_grad = input_grad.reshape(slots, length, width)

    def weight_of(k):
        rows = [pair[k * LANES : (k + 1) * LANES], last[group + k * extra : group + (k + 1) * extra]]
        return jnp.concatenate(rows, 0).T

    def bias_of(k):
        start = k * LANES
        return jnp.concatenate([sums[7, start : start + LANES], sums[7, span + start : span + start + extra]])

    return (
        output,
        input_grad,
        weight_of(0),
        bias_of(0),
        weight_of(1),
        weight_of(2),
        bias_of(2),
        last[:group],
        sums[2],
        sums[4],
        sums[5],
        sums[0],
        sums[1],
        totals[0],
        sums[6],
        totals[1],
        sums[3],
    )


def solution(mesh):
    dp, tp = mesh.shape["dp"], mesh.shape["tp"]
    placed = (
        P("dp", None, None),
        P("dp"),
        P(None, "tp"),
        P("tp"),
        P(None, "tp"),
        P(None, "tp"),
        P("tp"),
        P("tp", None),
        P(),
        P(),
        P(),
        P(),
        P(),
        P(None, "tp"),
        P("tp"),
        P("tp", None),
        P(),
        P("dp", None, None),
    )
    return jax.shard_map(
        partial(local, dp, tp),
        mesh=mesh,
        in_specs=placed,
        out_specs=(
            P("dp", None, None),
            P("dp", None, None),
            P(None, "tp"),
            P("tp"),
            P(None, "tp"),
            P(None, "tp"),
            P("tp"),
            P("tp", None),
            P(),
            P(),
            P(),
            P(),
            P(),
            P(None, "tp"),
            P("tp"),
            P("tp", None),
            P(),
        ),
        check_vma=False,
    )
```

```python
from functools import partial

import jax
import jax.numpy as jnp
from jax import lax
from jax.experimental import pallas as pl
from jax.experimental.pallas import tpu as pltpu
from jax.sharding import PartitionSpec as P

HEAD_DIM = 64
SHORT = 864
ROWS = 384
BLOCK = 256
LANES = 128
WIDE = 256
EPS = 1e-06
LOG2E = 1.4426950408889634
LN2 = 0.6931471805599453
BF16 = jnp.bfloat16
F32 = jnp.float32

NN = (((1,), (0,)), ((), ()))
NT = (((1,), (1,)), ((), ()))
TN = (((0,), (0,)), ((), ()))


def dot(left, right, dims):
    return lax.dot_general(left, right, dims, preferred_element_type=F32)


def shape_of(shape, dtype):
    return jax.ShapeDtypeStruct(shape, dtype)


def hbm_shape(shape, dtype):
    return pltpu.HBM(shape, dtype)


def run(body, scalars, grid, in_specs, out_specs, out_shape, scratch=(), alias=None, name=None, room=20):
    def call(*arrays):
        return pl.pallas_call(
            body,
            grid_spec=pltpu.PrefetchScalarGridSpec(
                num_scalar_prefetch=2,
                grid=grid,
                in_specs=in_specs,
                out_specs=out_specs,
                scratch_shapes=list(scratch),
            ),
            out_shape=out_shape,
            input_output_aliases={k + 2: v for k, v in (alias or {}).items()},
            compiler_params=pltpu.CompilerParams(vmem_limit_bytes=room << 20),
            cost_estimate=pl.CostEstimate(flops=1000, transcendentals=0, bytes_accessed=1000),
            name=name,
        )(*scalars, *arrays)

    return call


def in_hbm(v):
    return pltpu.with_memory_space_constraint(v, pltpu.HBM)


def whole(shape):
    return pl.BlockSpec(shape, lambda i, s, n: (0,) * len(shape))


def rows_of(width, at=0):
    return pl.BlockSpec((ROWS, width), lambda i, s, n: (i, at))


def cube_rows(width):
    return pl.BlockSpec((1, ROWS, width), lambda i, s, n: (s[0], i, 0))


def normalize(values):
    center = values - jnp.mean(values, -1, keepdims=True)
    inverse = lax.rsqrt(jnp.mean(center * center, -1, keepdims=True) + EPS)
    return center * inverse, inverse


def norm_back(grad, normal, inverse, gain):
    scaled = grad * gain
    return inverse * (
        scaled
        - jnp.mean(scaled, -1, keepdims=True)
        - normal * jnp.mean(scaled * normal, -1, keepdims=True)
    )


def column_sums(values):
    return jnp.sum(values, 0, keepdims=True)


def sum_rows(values):
    return dot(jnp.ones((8, values.shape[0]), BF16), values, NN)[0:1]


def accumulate(ref, value):
    first = pl.program_id(0) == 0

    @pl.when(first)
    def _():
        ref[...] = value

    @pl.when(jnp.logical_not(first))
    def _():
        ref[...] += value


SCALE = HEAD_DIM**-0.5 * LOG2E


def scaled(part):
    lane = lax.broadcasted_iota(jnp.int32, (1, part.shape[1]), 1)
    return (part * jnp.where(lane < LANES, SCALE, 1.0)).astype(BF16)


def pack_body(s, n, query, key, value, up, down, g1, s1, g2, s2, ob, db, ub, qb, vb, sent, third, params, lead, rest, sems):
    extra = query.shape[0] - LANES
    copies = []

    def move(source, target):
        copies.append(pltpu.make_async_copy(source, target, sems.at[len(copies)]))
        copies[-1].start()

    def pick(weight, act):
        count = lead.shape[0]
        for k, (start, target) in enumerate(((0, lead), (count, rest))):
            act(pltpu.make_async_copy(weight.at[pl.ds(start, target.shape[0])], target, sems.at[10 + k]))

    @pl.when(s[2] == 0)
    def _():
        pick(up, lambda copy: copy.start())

    @pl.when(s[2] != 0)
    def _():
        pick(down, lambda copy: copy.start())

    for k, weight in enumerate((query, key, value)):
        last = weight.at[pl.ds(LANES, extra)]
        move(weight.at[pl.ds(0, LANES)], sent.at[pl.ds(k * LANES, LANES)])
        move(last, sent.at[pl.ds(3 * LANES + k * extra, extra)])
        move(last, third.at[pl.ds(k * LANES, extra)])
    for k in range(3):
        third[k * LANES + extra : (k + 1) * LANES] = jnp.zeros((LANES - extra, third.shape[1]), BF16)
    table = [v[...].astype(F32).reshape(1, -1) for v in (g1, s1, g2, s2, ob, db, ub)]
    query_bias, value_bias = (v[...].astype(F32).reshape(1, -1) for v in (qb, vb))
    hole = jnp.zeros((1, LANES), F32)
    gap = jnp.zeros((1, LANES - extra), F32)
    ends = [jnp.concatenate([v[:, LANES:], gap], 1) for v in (query_bias, value_bias)]
    table.append(jnp.concatenate([query_bias[:, :LANES], hole, value_bias[:, :LANES], ends[0], hole, ends[1]], 1))
    table = jnp.concatenate(table, 0)
    params[...] = table
    sent[3 * LANES + 3 * extra :] = jnp.concatenate([table, table], 0).astype(BF16)
    for copy in copies:
        copy.wait()
    pick(up, lambda copy: copy.wait())


def first_body(s, n, tokens, params, pair_weight, third_weight, normed_out, pair_out, third_out):
    normal, _ = normalize(tokens[0].astype(F32))
    normed = (normal * params[0:1] + params[1:2]).astype(BF16)
    normed_out[...] = normed
    span = pair_weight.shape[0]
    pair_out[...] = scaled(dot(normed, pair_weight[...], NT) + params[7:8, :span])
    third_out[...] = scaled(dot(normed, third_weight[...], NT) + params[7:8, span:])


def head_view(ref, rows, start, head, heads):
    value = ref[rows, start : start + LANES]
    if heads == 1:
        return value
    lane = lax.broadcasted_iota(jnp.int32, (1, LANES), 1)
    keep = (lane < HEAD_DIM) if head == 0 else (lane >= HEAD_DIM)
    return jnp.where(keep, value, jnp.zeros((), BF16))


def pick_head(values):
    if len(values) == 1:
        return values[0]
    lane = lax.broadcasted_iota(jnp.int32, (1, LANES), 1)
    return jnp.where(lane < HEAD_DIM, values[0], values[1])


def attend_part(queries, sources, attended, logsum, limit, block):
    count = queries[0].shape[0] // block
    keys = [source[:limit, LANES : 2 * LANES] for source in sources]
    values = [source[:limit, 2 * LANES :] for source in sources]

    def scores(unit):
        at, head = unit
        rows = slice(at * block, (at + 1) * block)
        return dot(head_view(queries[head // 2], rows, 0, head, 2 - head // 2), keys[head // 2], NT)

    units = [(at, head) for at in range(count) for head in range(3)]
    current = scores(units[0])
    done = []
    for index, (at, head) in enumerate(units):
        following = scores(units[index + 1]) if index + 1 < len(units) else None
        peak = jnp.max(current, -1, keepdims=True)
        expo = jnp.exp2(current - peak)
        total = jnp.sum(expo, -1, keepdims=True)
        mixed = dot(expo.astype(BF16), values[head // 2], NN)
        done.append((mixed * (1.0 / total), jnp.broadcast_to(peak + jnp.log2(total), mixed.shape)))
        current = following
        if head == 2:
            rows = slice(at * block, (at + 1) * block)
            attended[rows, :LANES] = pick_head([done[0][0], done[1][0]]).astype(BF16)
            attended[rows, LANES:] = done[2][0].astype(BF16)
            table = jnp.transpose(pick_head([done[0][1], done[1][1]]))
            logsum[:8, rows] = jnp.concatenate([table[0:4], table[HEAD_DIM : HEAD_DIM + 4]], 0)
            logsum[8:, rows] = jnp.transpose(done[2][1])[:8]
            done = []


def attend_body(s, n, query_pair, query_third, pair, third, attended, logsum):
    full = pair.shape[0]

    @pl.when(n[s[0]] == full)
    def _():
        attend_part((query_pair, query_third), (pair, third), attended, logsum, full, BLOCK)

    @pl.when(n[s[0]] != full)
    def _():
        attend_part((query_pair, query_third), (pair, third), attended, logsum, SHORT, BLOCK)


def attend_back_part(qkv, grad, logsum, inner, grads, heads, limit, block, full):
    count = -(-limit // block)
    keys = qkv[:limit, LANES : 2 * LANES]
    values = qkv[:limit, 2 * LANES :]

    def span(at):
        return slice(at * block, min((at + 1) * block, limit))

    def front(unit):
        head, at = unit
        query = head_view(qkv, span(at), 0, head, heads)
        pull = head_view(grad, span(at), 0, head, heads)
        return dot(keys, query, NT), dot(values, pull, NT), query, pull

    def put(rows, start, head, value):
        value = value.astype(BF16)
        if head == 1:
            value = pick_head([grads[rows, start : start + LANES], value])
        grads[rows, start : start + LANES] = value

    units = [(head, at) for head in range(heads) for at in range(count)]
    current = front(units[0])
    for index, (head, at) in enumerate(units):
        following = front(units[index + 1]) if index + 1 < len(units) else None
        scores, grad_probs, query, pull = current
        at_row = slice(4 * head, 4 * head + 1)
        probs = jnp.exp2(scores - logsum[at_row, span(at)])
        grad_scores = (probs * (grad_probs - inner[at_row, span(at)])).astype(BF16)
        value_part = dot(probs.astype(BF16), pull, NN)
        key_part = dot(grad_scores, query, NN)
        grad_values = value_part if at == 0 else grad_values + value_part
        grad_keys = key_part if at == 0 else grad_keys + key_part
        put(span(at), 0, head, dot(grad_scores, keys, TN) * HEAD_DIM**-0.5)
        if at == count - 1:
            put(slice(0, limit), LANES, head, grad_keys * LN2)
            put(slice(0, limit), 2 * LANES, head, grad_values)
        current = following
    if limit < full:
        grads[limit:, :] = jnp.zeros((full - limit, grads.shape[1]), BF16)


def attend_back_body(heads, s, n, qkv, grad, logsum, inner, grads):
    full = qkv.shape[0]

    @pl.when(n[s[0]] == full)
    def _():
        attend_back_part(qkv, grad, logsum, inner, grads, heads, full, BLOCK, full)

    @pl.when(n[s[0]] != full)
    def _():
        attend_back_part(qkv, grad, logsum, inner, grads, heads, SHORT, BLOCK, full)


def middle_body(s, n, tokens, params, *refs):
    arrays, weights, (middle_out, normed_out) = refs[:4], refs[4:8], refs[8:]
    branch = params[4:5]
    for array, weight in zip(arrays, weights):
        branch = branch + dot(array[:, : weight.shape[0]], weight[...], NN)
    middle = tokens[0].astype(F32) + branch
    middle_out[...] = middle.astype(BF16)
    normal, _ = normalize(middle)
    normed_out[...] = (normal * params[2:3] + params[3:4]).astype(BF16)


def gelu_and_slope(values):
    t = 1.0 / (1.0 + (0.3275911 * 0.7071067811865476) * jnp.abs(values))
    series = t * (
        (0.5 * 0.254829592)
        + t * ((0.5 * -0.284496736) + t * ((0.5 * 1.421413741) + t * ((0.5 * -1.453152027) + t * (0.5 * 1.061405429))))
    )
    decay = jnp.exp2(values * values * (-0.5 * LOG2E))
    tail = series * decay
    share = jnp.where(values >= 0, 1.0 - tail, tail)
    return values * share, share + values * (decay * 0.3989422804014327)


def hidden_part(normed, grad_feed, up, down, bias, active_out, upper_out, bias_out, put):
    block = normed.shape[0]
    count = 1

    def front(at):
        rows = slice(at * block, (at + 1) * block)
        return dot(normed[rows], up[...], NN), dot(grad_feed[rows], down[...], NT)

    current = front(0)
    total = None
    for at in range(count):
        following = front(at + 1) if at + 1 < count else None
        rows = slice(at * block, (at + 1) * block)
        active, slope = gelu_and_slope(current[0] + bias)
        active = active.astype(BF16)
        active_out[rows] = active
        grad_upper = (current[1] * slope).astype(BF16)
        upper_out[rows] = grad_upper
        put(rows, dot(active, down[...], NN), dot(grad_upper, up[...], NT))
        sums = sum_rows(grad_upper)
        total = sums if total is None else total + sums
        current = following
    accumulate(bias_out, total)


def hidden_own_body(s, n, normed, cot, up, down, params, feed_grad_out, active_out, upper_out, feed_out, back_out, bias_out):
    position = pl.program_id(0) * ROWS + lax.broadcasted_iota(jnp.int32, (ROWS, 1), 0)
    grad_feed = jnp.where(position < n[s[0]], cot[0], jnp.zeros((), BF16))
    feed_grad_out[...] = grad_feed

    def put(rows, feed, back):
        feed_out[rows] = feed.astype(BF16)
        back_out[rows] = back.astype(BF16)

    hidden_part(normed[...], grad_feed, up, down, params[6:7], active_out, upper_out, bias_out, put)


def hidden_far_body(s, n, normed, grad_feed, feed_in, back_in, g0, g1, o0, o1, small, *refs):
    (active_out, upper_out, feed_out, back_out, bias_out), (up, down, sems) = refs[:5], refs[5:]
    part = g0.shape[0]

    @pl.when(pl.program_id(0) == 0)
    def _():
        def fill(first, second):
            copies = []
            for at, (target, sources) in enumerate(((up, first), (down, second))):
                rows = (pl.ds(0, part), pl.ds(part, target.shape[0] - part))
                for k, source in enumerate(sources):
                    copies.append(pltpu.make_async_copy(source, target.at[rows[k]], sems.at[2 * at + k]))
            for copy in copies:
                copy.start()
            for copy in copies:
                copy.wait()

        @pl.when(s[2] == 0)
        def _():
            fill((g0, g1), (o0, o1))

        @pl.when(s[2] != 0)
        def _():
            fill((o0, o1), (g0, g1))

    def put(rows, feed, back):
        feed_out[rows] = (feed_in[rows].astype(F32) + feed).astype(BF16)
        back_out[rows] = (back_in[rows].astype(F32) + back).astype(BF16)

    hidden_part(normed[...], grad_feed[...], up, down, small[6:7].astype(F32), active_out, upper_out, bias_out, put)


def output_body(s, n, middle, feed, side, params, own_out):
    total = feed[...].astype(F32) + side[...].astype(F32)
    own_out[...] = (middle[...].astype(F32) + total + params[5:6]).astype(BF16)


def split_body(s, n, whole_in, *outs):
    count = outs[0].shape[0]
    mine = 2 * s[4] + s[5]
    for k, out in enumerate(outs):
        start = pl.multiple_of((mine ^ k) * count, 8)
        out[...] = whole_in[pl.ds(start, count)]


def second_body(s, n, *refs):
    up, down = refs[:4], refs[4:8]
    outs = refs[8:]
    for (near, got_near, away, got_away), bit, (kept, sent) in ((up, s[5], outs[:2]), (down, s[4], outs[2:])):
        count = kept.shape[1]
        for k, (own, got) in enumerate(((near, got_near), (away, got_away))):
            for target, half in ((kept, bit), (sent, 1 - bit)):
                rows = pl.ds(pl.multiple_of(half * count, 8), count)
                target[k] = (own[rows].astype(F32) + got[rows].astype(F32)).astype(BF16)


def third_body(s, n, up, got_up, down, got_down, up_out, down_out, sent):
    count = up.shape[1]
    for k, (own, got, out) in enumerate(((up, got_up, up_out), (down, got_down, down_out))):
        out[...] = (own[0].astype(F32) + got[0].astype(F32)).astype(BF16)
        sent[k * count : (k + 1) * count] = (own[1].astype(F32) + got[1].astype(F32)).astype(BF16)


def gather_body(flips, s, n, *refs):
    for j, (out, flip) in enumerate(zip(refs[4 * len(flips) :], flips)):
        count = out.shape[0] // 4
        for k in range(4):
            high, low = (s[5] ^ (k % 2), s[4] ^ (k // 2)) if flip else (s[4] ^ (k // 2), s[5] ^ (k % 2))
            out[pl.ds(pl.multiple_of((2 * high + low) * count, 8), count)] = refs[4 * j + k][...].astype(F32)


def assemble_body(places, s, n, *refs):
    pieces, result, sems = refs[: len(places)], refs[-2], refs[-1]
    copies = []
    for k, ((where, start), piece) in enumerate(zip(places, pieces)):
        target = result.at[s[3] ^ where, pl.ds(start, piece.shape[0])]
        copies.append(pltpu.make_async_copy(piece, target, sems.at[k]))
        copies[-1].start()
    for copy in copies:
        copy.wait()


def back_two_body(s, n, middle, grad_feed, g0, g1, params, w0, w1, a0, a1, branch_out, *refs):
    grad_tiles, inner_outs, sums_out = refs[:4], refs[4:8], refs[8]
    normal, inverse = normalize(middle[...].astype(F32))
    grad_normed = g0[...].astype(F32) + g1[...].astype(F32)
    grad_output = grad_feed[...].astype(F32)
    grad_middle = grad_output + norm_back(grad_normed, normal, inverse, params[2:3])
    grad_branch = grad_middle.astype(BF16)
    branch_out[...] = grad_branch
    sums = jnp.concatenate(
        [
            column_sums(grad_normed * normal),
            column_sums(grad_normed),
            column_sums(grad_branch.astype(F32)),
            column_sums(grad_output),
        ],
        0,
    )
    accumulate(sums_out, sums)
    lane = lax.broadcasted_iota(jnp.int32, (8, LANES), 1)
    head = lax.broadcasted_iota(jnp.int32, (8, LANES), 0)
    member = (lane // HEAD_DIM == head // 4).astype(BF16)
    for k, (weight, array) in enumerate(((w0, a0), (w1, a1))):
        grad_att = dot(grad_branch, weight[...], NT).astype(BF16)
        extra = grad_att.shape[1] - LANES
        gap = jnp.zeros((grad_att.shape[0], LANES - extra), BF16)
        for t in range(2):
            lanes = slice(t * LANES, (t + 1) * LANES)
            part = grad_att[:, :LANES] if t == 0 else jnp.concatenate([grad_att[:, LANES:], gap], 1)
            grad_tiles[2 * k + t][...] = part
            product = part.astype(F32) * array[:, lanes].astype(F32)
            high = product.astype(BF16)
            low = (product - high.astype(F32)).astype(BF16)
            inner_outs[2 * k + t][...] = dot(member, high, NT) + dot(member, low, NT)


def back_one_body(s, n, tokens, grad_middle, g0, g1, g2, g3, params, own_out, sums_out):
    normal, inverse = normalize(tokens[0].astype(F32))
    grad_normed = (g0[...].astype(F32) + g1[...].astype(F32)) + (g2[...].astype(F32) + g3[...].astype(F32))
    accumulate(
        sums_out, jnp.concatenate([column_sums(grad_normed * normal), column_sums(grad_normed)], 0)
    )
    back = norm_back(grad_normed, normal, inverse, params[0:1])
    own_out[...] = (grad_middle[...].astype(F32) + back).astype(BF16)


def pairs(count, mask):
    return [(i, i ^ mask) for i in range(count)]


def overlap(moves, kernel=None, inputs=()):
    operands, inputs = lax.optimization_barrier((tuple(v for _, v in moves), tuple(inputs)))
    received = tuple(move(v) for (move, _), v in zip(moves, operands))
    results = tuple(kernel(*inputs)) if kernel else ()
    return lax.optimization_barrier((received, results))


def after(value, *others):
    return lax.optimization_barrier((value, *others))[0]


def local(
    dp, tp,
    tokens, cube_lengths, query_weight, query_bias, key_weight, value_weight, value_bias,
    out_weight, out_bias, first_gain, first_shift, second_gain, second_shift,
    up_weight, up_bias, down_weight, down_bias, cotangent,
):
    slots, length, width = tokens.shape
    group = query_weight.shape[1]
    hidden = up_weight.shape[1]
    blocks = length // ROWS
    half = length // 2
    half_rows = half // 2
    mine = lax.axis_index("tp")
    place = lax.axis_index("dp")
    cube, core = mine // 2, mine % 2
    parity = place & 1
    bits = [1 << k for k in range(dp.bit_length() - 1)]
    scalars = (jnp.stack([cube, core, parity, mine, parity, (place // 2) & 1]).astype(jnp.int32), cube_lengths)

    def to_core(v):
        return lax.ppermute(v, "tp", pairs(tp, 1))

    def to_chip(v):
        return lax.ppermute(v, "tp", pairs(tp, 2))

    def to_place(v, mask):
        return lax.ppermute(v, "dp", pairs(dp, mask))

    full = (length, width)
    span = 3 * LANES
    extra = group - LANES
    vectors = whole((8, width))
    part_spec = whole((span, width))
    part_shape = shape_of((length, span), BF16)

    top = span + 3 * extra
    far_shape = (top + 16, width)
    anywhere = pl.BlockSpec(memory_space=pl.ANY)
    vector = pl.BlockSpec((width,), lambda i, s, n: (0,))
    short_vector = pl.BlockSpec((group,), lambda i, s, n: (0,))
    lead_rows = (2 * hidden // 3) // LANES * LANES
    sent, third_0, params, lead, rest = run(
        pack_body, scalars, (1,),
        [anywhere] * 5 + [vector] * 7 + [short_vector] * 2,
        [whole(far_shape), part_spec, vectors, whole((lead_rows, width)), whole((hidden - lead_rows, width))],
        [shape_of(far_shape, BF16), shape_of((span, width), BF16), shape_of((8, width), F32),
         shape_of((lead_rows, width), BF16), shape_of((hidden - lead_rows, width), BF16)],
        scratch=[pltpu.SemaphoreType.DMA((12,))],
        name="pack_weights", room=10,
    )(
        *map(in_hbm, (
            query_weight.T, key_weight.T, value_weight.T, up_weight, down_weight,
            first_gain, first_shift, second_gain, second_shift, out_bias, down_bias, up_bias, query_bias, value_bias,
        ))
    )
    far = to_chip(sent)

    def spread(rows):
        gap = ((0, 0), (0, LANES - extra), (0, 0))
        return jnp.pad(rows.reshape(3, extra, width), gap).reshape(span, width)

    normed, part_0, part_1 = run(
        first_body, scalars, (blocks,),
        [cube_rows(width), vectors, part_spec, part_spec],
        [rows_of(width), rows_of(span), rows_of(span)],
        [shape_of(full, BF16), part_shape, part_shape],
        name="first_norm_project", room=10,
    )(in_hbm(tokens), params, sent, third_0)
    pair_0 = sent[:span]

    def attend(pair, third):
        step = length // 2
        query = pl.BlockSpec((step, LANES), lambda i, s, n: (i, 0))
        return run(
            attend_body, scalars, (2,),
            [query, query, whole((length, span)), whole((length, span))],
            [pl.BlockSpec((step, 2 * LANES), lambda i, s, n: (i, 0)), pl.BlockSpec((16, step), lambda i, s, n: (0, i))],
            [shape_of((length, 2 * LANES), BF16), shape_of((16, length), F32)],
            name="attend", room=14,
        )(pair, third, pair, third)

    def project(weight, bias, at):
        return scaled(dot(normed, weight, NT) + bias[:, at * span : (at + 1) * span])

    att_0, log_0 = attend(part_0, part_1)
    far = after(far, att_0)
    pair_1, third_1 = far[:span], spread(far[span:top])
    bias_1 = far[top + 7 : top + 8].astype(F32)
    part_2 = project(pair_1, bias_1, 0)
    part_3 = project(third_1, bias_1, 1)
    got_0 = to_chip(after(lead, far))
    (side_0, out_far), (att_1, log_1) = overlap([(to_core, att_0), (to_chip, out_weight)], attend, (part_2, part_3))
    out_side = to_core(jnp.concatenate([out_weight, out_far], 0))
    side_1 = to_core(att_1)

    double_tile = rows_of(2 * LANES)

    def out_block(at):
        return pl.BlockSpec((group, width), lambda i, s, n: (at, 0))

    out_specs = [out_block(0), out_block(0), out_block(0), out_block(1)]
    middle, normed_two = run(
        middle_body, scalars, (blocks,),
        [cube_rows(width), vectors] + [double_tile] * 4 + out_specs,
        [rows_of(width)] * 2,
        [hbm_shape(full, BF16), shape_of(full, BF16)],
        name="attention_out_norm", room=12,
    )(in_hbm(tokens), params, att_0, att_1, side_0, side_1, out_weight, out_far, out_side, out_side)

    own_spec = pl.BlockSpec((half_rows, width), lambda i, s, n: (s[1] * 2 + i, 0))
    plain = pl.BlockSpec((half_rows, width), lambda i, s, n: (i, 0))
    own_shape = shape_of((half, width), BF16)

    def assemble(pieces):
        return run(
            partial(assemble_body, tuple(place for place, _ in pieces)), scalars, (1,),
            [whole(piece.shape) for _, piece in pieces], [anywhere], [shape_of((tp, half, width), BF16)],
            scratch=[pltpu.SemaphoreType.DMA((len(pieces),))],
            name="assemble", room=12,
        )(*(piece for _, piece in pieces))[0].reshape(slots, length, width)

    def side_half(v):
        return lax.dynamic_slice(v, ((1 - core) * half, 0), (half, v.shape[1]))

    def bit_of(mask):
        return (place // mask) & 1

    def half_at(v, bit):
        count = v.shape[-2] // 2
        return lax.dynamic_slice_in_dim(v, bit * count, count, v.ndim - 2)

    def half_out(v, mask):
        return half_at(v, 1 - bit_of(mask))

    def half_kept(v, mask):
        return half_at(v, bit_of(mask))

    def add(a, b):
        return (a.astype(F32) + b.astype(F32)).astype(BF16)

    def join(v, other, mask):
        return jnp.where(bit_of(mask) == 0, jnp.concatenate([v, other], 0), jnp.concatenate([other, v], 0))

    both = shape_of((length, hidden), BF16)
    hidden_shapes = [both, both, hbm_shape(full, BF16), shape_of(full, BF16), shape_of((1, hidden), F32)]

    hidden_specs = [rows_of(hidden), rows_of(hidden), rows_of(width), rows_of(width), whole((1, hidden))]

    own_call = run(
        hidden_own_body, scalars, (blocks,),
        [rows_of(width), cube_rows(width), whole((width, hidden)), whole((hidden, width)), vectors],
        [rows_of(width)] + hidden_specs,
        [shape_of(full, BF16)] + hidden_shapes,
        name="hidden_own", room=16,
    )
    (got_1, other_0), (grad_feed, active_0, upper_0, feed, back, up_bias_0) = overlap(
        [(to_chip, rest), (partial(to_place, mask=1), got_0)],
        own_call,
        (normed_two, in_hbm(cotangent), in_hbm(up_weight), in_hbm(down_weight), params),
    )
    other_1 = to_place(got_1, 1)

    def hidden_grads(active, upper):
        return dot(normed_two, upper, TN).astype(BF16), dot(active, grad_feed, TN).astype(BF16)

    near = hidden_grads(active_0, upper_0)
    orders = [bits, bits[1:2] + bits[:1] + bits[2:]]
    far_call = run(
        hidden_far_body, scalars, (blocks,),
        [rows_of(width)] * 4 + [anywhere] * 4 + [pl.BlockSpec((16, width), lambda i, s, n: (top // 16, 0))],
        hidden_specs,
        hidden_shapes,
        scratch=[pltpu.VMEM((width, hidden), BF16), pltpu.VMEM((hidden, width), BF16), pltpu.SemaphoreType.DMA((4,))],
        name="hidden_far", room=16,
    )

    square = [bits[1], bits[0], bits[0] | bits[1]]

    def quarters(v):
        piece = (v.shape[0] // 4, v.shape[1])
        return run(
            split_body, scalars, (1,), [whole(v.shape)], [whole(piece)] * 4, [shape_of(piece, BF16)] * 4, name="split", room=8
        )(v)

    def gather(pieces, flips):
        shapes = [(4 * pieces[4 * j].shape[0], width) for j in range(len(flips))]
        return run(
            partial(gather_body, flips), scalars, (1,), [whole(piece.shape) for piece in pieces], [whole(shape) for shape in shapes],
            [shape_of(shape, F32) for shape in shapes], name="gather", room=16,
        )(*pieces)

    def to_square(pieces):
        return [(partial(to_place, mask=mask), v) for mask, v in zip(square, pieces)]

    sent_near = [half_out(v, order[0]) for v, order in zip(near, orders)]

    def over(order, k):
        return lambda v: to_place(v, order[k])

    got_near, (active_1, upper_1, feed, back, up_bias_1) = overlap(
        [(over(order, 0), v) for v, order in zip(sent_near, orders)],
        far_call,
        (normed_two, grad_feed, feed, back, got_0, got_1, other_0, other_1, far),
    )
    side_back = to_core(back)
    side_feed = to_core(side_half(feed))
    away = hidden_grads(active_1, upper_1)
    (own_output,) = run(
        output_body, scalars, (2,),
        [own_spec] * 2 + [plain, vectors],
        [plain], [own_shape], name="output", room=8,
    )(after(middle, *away), feed, side_feed, params)
    sent_away = [half_out(v, order[0]) for v, order in zip(away, orders)]

    tile = rows_of(LANES)
    tile_shape = hbm_shape((length, LANES), BF16)
    inner_shape = hbm_shape((8, length), F32)
    two_call = run(
        back_two_body, scalars, (blocks,),
        [rows_of(width)] * 4 + [vectors] + out_specs[:2] + [double_tile] * 2,
        [rows_of(width)] + [tile] * 4 + [pl.BlockSpec((8, ROWS), lambda i, s, n: (0, i))] * 4 + [whole((4, width))],
        [hbm_shape(full, BF16)] + [tile_shape] * 4 + [inner_shape] * 4 + [shape_of((4, width), F32)],
        name="second_norm_back", room=13,
    )
    (far_output_0, side_output, *got_away), results = overlap(
        [(to_chip, own_output[:half_rows]), (to_core, own_output)] + [(over(order, 0), v) for v, order in zip(sent_away, orders)],
        two_call,
        (middle, in_hbm(grad_feed), back, side_back, params, out_weight, out_far, in_hbm(att_0), in_hbm(att_1)),
    )
    grad_branch, gt_0, gt_1, gt_2, gt_3, in_0, in_1, in_2, in_3, sums_two = results

    def attend_back(qkv, grad, logsum, inner, count):
        at = 2 - count
        return run(
            partial(attend_back_body, count), scalars, (1,),
            [whole((length, span)), whole((length, LANES)), pl.BlockSpec((8, length), lambda i, s, n: (at, 0)), whole((8, length))],
            [whole((length, span))],
            [part_shape],
            name="attend_back", room=13,
        )(qkv, grad, logsum, inner)

    def weight_grad(grads):
        return dot(grads, normed, TN).astype(BF16)

    def third_only(v):
        return v.reshape(3, LANES, width)[:, :extra].reshape(3 * extra, width)

    pair_back, third_back = partial(attend_back, count=2), partial(attend_back, count=1)
    second_half = hidden // 2
    kept_rows = [pl.BlockSpec((second_half, width), lambda i, s, n: (s[4], 0)), pl.BlockSpec((second_half, width), lambda i, s, n: (s[5], 0))]
    piece = whole((second_half, width))
    two_shape = (2, second_half // 2, width)
    up_kept, up_sent, down_kept, down_sent = run(
        second_body, scalars, (1,),
        [kept_rows[0], piece, kept_rows[0], piece, kept_rows[1], piece, kept_rows[1], piece],
        [whole(two_shape)] * 4, [shape_of(two_shape, BF16)] * 4, name="second_halving", room=12,
    )(near[0], got_near[0], away[0], got_away[0], near[1], got_near[1], away[1], got_away[1])
    sent_2 = [up_sent, down_sent]
    (far_output_1, across_output_0, *got_second), (grads_2,) = overlap(
        [(to_chip, own_output[half_rows:]), (to_core, far_output_0)] + [(over(order, 1), v) for v, order in zip(sent_2, orders)],
        pair_back,
        (part_2, gt_2, log_1, in_2),
    )
    quarter_shape = (second_half // 2, width)
    up_third, down_third, sent_3 = run(
        third_body, scalars, (1,),
        [whole(two_shape)] * 4, [whole(quarter_shape)] * 2 + [piece],
        [shape_of(quarter_shape, BF16)] * 2 + [shape_of((second_half, width), BF16)], name="third_sum", room=10,
    )(up_kept, got_second[0], down_kept, got_second[1])
    (across_output_1, got_third), (grads_0,) = overlap(
        [(to_core, far_output_1), (to_chip, sent_3)], pair_back, (part_0, gt_0, log_0, in_0)
    )
    output = assemble([
        ((0, 0), own_output), ((1, 0), side_output), ((2, 0), far_output_0), ((2, half_rows), far_output_1),
        ((3, 0), across_output_0), ((3, half_rows), across_output_1),
    ])
    out_grads = [dot(a, grad_branch, TN).astype(BF16)[:group] for a in (att_0, att_1)]
    quarter = got_third.shape[0] // 2
    stage_4 = [add(v, got_third[k * quarter : (k + 1) * quarter]) for k, v in enumerate((up_third, down_third))]
    pair_away = weight_grad(grads_2)
    back_most = dot(grads_2, pair_1, NN) + dot(grads_0, pair_0, NN)
    (pair_far, got_up), (grads_3,) = overlap(
        [(to_chip, pair_away), (over(bits, 2), stage_4[0])], third_back, (part_3, gt_3, log_1, in_3)
    )
    third_away = third_only(weight_grad(grads_3))
    back_most = (back_most + dot(grads_3, third_1, NN)).astype(BF16)
    side_most_sent = side_half(back_most)
    pair = add(weight_grad(grads_0), pair_far)
    sent_pair = half_out(pair, bits[0])
    last_away = jnp.concatenate([out_grads[1], third_away], 0)
    (got_pair, last_far, side_most, got_down), (grads_1,) = overlap(
        [(over(bits, 0), sent_pair), (to_chip, last_away), (to_core, side_most_sent), (over(bits, 2), stage_4[1])],
        third_back,
        (part_1, gt_1, log_0, in_1),
    )
    back_last = dot(grads_1, third_0, NN).astype(BF16)
    side_last = to_core(side_half(back_last))
    last = add(jnp.concatenate([out_grads[0], third_only(weight_grad(grads_1))], 0), last_far)
    last_pieces = quarters(last)
    pair = add(half_kept(pair, bits[0]), got_pair)
    sent_pair = half_out(pair, bits[1])
    totals = [add(v, g) for v, g in zip(stage_4, (got_up, got_down))]
    for mask in bits[3:]:
        totals = [add(v, to_place(v, mask)) for v in totals]

    token_spec = pl.BlockSpec((1, half_rows, width), lambda i, s, n: (s[0], s[1] * 2 + i, 0))
    one_call = run(
        back_one_body, scalars, (2,),
        [token_spec, own_spec, own_spec, own_spec, plain, plain, vectors],
        [plain, whole((2, width))],
        [own_shape, shape_of((2, width), F32)],
        name="first_norm_back", room=14,
    )
    (got_pair, *got_last), (own_grad, sums_one) = overlap(
        [(over(bits, 1), sent_pair)] + to_square(last_pieces[1:]),
        one_call,
        (in_hbm(tokens), in_hbm(grad_branch), back_most, back_last, side_most, side_last, params),
    )
    last = sum((g.astype(F32) for g in got_last), last_pieces[0].astype(F32)).astype(BF16)
    pair = add(half_kept(pair, bits[1]), got_pair)
    mixed = jnp.concatenate([pair, last], 0)

    (far_0, side_grad, up_near, down_near, first_sums), _ = overlap(
        [(to_chip, own_grad[:half_rows]), (to_core, own_grad)]
        + [(over(order, 1), v) for v, order in zip(totals, orders)]
        + [(to_core, sums_one)]
    )
    first_sums = sums_one + first_sums

    def bias_sums(pair, third):
        return jnp.concatenate([sum_rows(pair), sum_rows(third)], 1)

    shared = [sums_two, first_sums]
    sums = jnp.concatenate(shared + [up_bias_0, bias_sums(grads_0, grads_1)], 0)
    sums_away = jnp.concatenate(shared + [up_bias_1, bias_sums(grads_2, grads_3)], 0)
    both_up, both_down = (jnp.concatenate([v, g], 0) for v, g in zip(totals, (up_near, down_near)))
    (far_1, up_other, down_other, got_mixed, got_sums), _ = overlap(
        [(to_chip, own_grad[half_rows:]), (over(bits, 0), both_up), (over(bits, 1), both_down), (over(bits, 2), mixed), (to_chip, sums_away)]
    )
    mixed = add(mixed, got_mixed)
    for mask in bits[3:]:
        mixed = add(mixed, to_place(mixed, mask))
    sums = sums + got_sums
    (*got_mixed, across_1, across_0), _ = overlap(to_square([mixed] * 3) + [(to_core, far_1), (to_core, far_0)])
    got_z, got_y, got_yz = overlap(to_square([sums] * 3))[0]
    sums = (sums + got_y) + (got_z + got_yz)
    for mask in bits[2:]:
        sums = sums + to_place(sums, mask)
    quarter = up_near.shape[0]
    up_total, down_total = gather(
        [totals[0], up_near, up_other[:quarter], up_other[quarter:], totals[1], down_other[:quarter], down_near, down_other[quarter:]],
        (False, True),
    )
    quarter = pair.shape[0]
    parts = [mixed, *got_mixed]
    pair, last = gather([v[:quarter] for v in parts] + [v[quarter:] for v in parts], (False, False))
    input_grad = assemble([
        ((0, 0), own_grad), ((1, 0), side_grad), ((2, 0), far_0), ((2, half_rows), far_1), ((3, 0), across_0), ((3, half_rows), across_1),
    ])

    def weight_of(k):
        rows = [pair[k * LANES : (k + 1) * LANES], last[group + k * extra : group + (k + 1) * extra]]
        return jnp.concatenate(rows, 0).T

    def bias_of(k):
        start = k * LANES
        return jnp.concatenate([sums[7, start : start + LANES], sums[7, span + start : span + start + extra]])

    return (
        output,
        input_grad,
        weight_of(0),
        bias_of(0),
        weight_of(1),
        weight_of(2),
        bias_of(2),
        last[:group],
        sums[2],
        sums[4],
        sums[5],
        sums[0],
        sums[1],
        up_total,
        sums[6],
        down_total,
        sums[3],
    )


def solution(mesh):
    dp, tp = mesh.shape["dp"], mesh.shape["tp"]
    placed = (
        P("dp", None, None),
        P("dp"),
        P(None, "tp"),
        P("tp"),
        P(None, "tp"),
        P(None, "tp"),
        P("tp"),
        P("tp", None),
        P(),
        P(),
        P(),
        P(),
        P(),
        P(None, "tp"),
        P("tp"),
        P("tp", None),
        P(),
        P("dp", None, None),
    )
    return jax.shard_map(
        partial(local, dp, tp),
        mesh=mesh,
        in_specs=placed,
        out_specs=(
            P("dp", None, None),
            P("dp", None, None),
            P(None, "tp"),
            P("tp"),
            P(None, "tp"),
            P(None, "tp"),
            P("tp"),
            P("tp", None),
            P(),
            P(),
            P(),
            P(),
            P(),
            P(None, "tp"),
            P("tp"),
            P("tp", None),
            P(),
        ),
        check_vma=False,
    )
```

```python
from functools import partial

import jax
import jax.numpy as jnp
from jax import lax
from jax.experimental import pallas as pl
from jax.experimental.pallas import tpu as pltpu
from jax.sharding import PartitionSpec as P

HEAD_DIM = 64
SHORT = 864
ROWS = 384
BLOCK = 256
LANES = 128
WIDE = 256
EPS = 1e-06
LOG2E = 1.4426950408889634
LN2 = 0.6931471805599453
BF16 = jnp.bfloat16
F32 = jnp.float32

NN = (((1,), (0,)), ((), ()))
NT = (((1,), (1,)), ((), ()))
TN = (((0,), (0,)), ((), ()))


def dot(left, right, dims):
    return lax.dot_general(left, right, dims, preferred_element_type=F32)


def shape_of(shape, dtype):
    return jax.ShapeDtypeStruct(shape, dtype)


def hbm_shape(shape, dtype):
    return pltpu.HBM(shape, dtype)


def run(body, scalars, grid, in_specs, out_specs, out_shape, scratch=(), alias=None, name=None, room=20):
    def call(*arrays):
        return pl.pallas_call(
            body,
            grid_spec=pltpu.PrefetchScalarGridSpec(
                num_scalar_prefetch=2,
                grid=grid,
                in_specs=in_specs,
                out_specs=out_specs,
                scratch_shapes=list(scratch),
            ),
            out_shape=out_shape,
            input_output_aliases={k + 2: v for k, v in (alias or {}).items()},
            compiler_params=pltpu.CompilerParams(vmem_limit_bytes=room << 20),
            cost_estimate=pl.CostEstimate(flops=1000, transcendentals=0, bytes_accessed=1000),
            name=name,
        )(*scalars, *arrays)

    return call


def in_hbm(v):
    return pltpu.with_memory_space_constraint(v, pltpu.HBM)


def whole(shape):
    return pl.BlockSpec(shape, lambda i, s, n: (0,) * len(shape))


def rows_of(width, at=0):
    return pl.BlockSpec((ROWS, width), lambda i, s, n: (i, at))


def cube_rows(width):
    return pl.BlockSpec((1, ROWS, width), lambda i, s, n: (s[0], i, 0))


def normalize(values):
    center = values - jnp.mean(values, -1, keepdims=True)
    inverse = lax.rsqrt(jnp.mean(center * center, -1, keepdims=True) + EPS)
    return center * inverse, inverse


def norm_back(grad, normal, inverse, gain):
    scaled = grad * gain
    return inverse * (
        scaled
        - jnp.mean(scaled, -1, keepdims=True)
        - normal * jnp.mean(scaled * normal, -1, keepdims=True)
    )


def column_sums(values):
    return jnp.sum(values, 0, keepdims=True)


def sum_rows(values):
    return dot(jnp.ones((8, values.shape[0]), BF16), values, NN)[0:1]


def accumulate(ref, value):
    first = pl.program_id(0) == 0

    @pl.when(first)
    def _():
        ref[...] = value

    @pl.when(jnp.logical_not(first))
    def _():
        ref[...] += value


SCALE = HEAD_DIM**-0.5 * LOG2E


def scaled(part):
    lane = lax.broadcasted_iota(jnp.int32, (1, part.shape[1]), 1)
    return (part * jnp.where(lane < LANES, SCALE, 1.0)).astype(BF16)


def pack_body(s, n, query, key, value, up, down, g1, s1, g2, s2, ob, db, ub, qb, vb, sent, third, params, lead, rest, sems):
    extra = query.shape[0] - LANES
    copies = []

    def move(source, target):
        copies.append(pltpu.make_async_copy(source, target, sems.at[len(copies)]))
        copies[-1].start()

    def pick(weight, act):
        count = lead.shape[0]
        for k, (start, target) in enumerate(((0, lead), (count, rest))):
            act(pltpu.make_async_copy(weight.at[pl.ds(start, target.shape[0])], target, sems.at[10 + k]))

    @pl.when(s[2] == 0)
    def _():
        pick(up, lambda copy: copy.start())

    @pl.when(s[2] != 0)
    def _():
        pick(down, lambda copy: copy.start())

    for k, weight in enumerate((query, key, value)):
        last = weight.at[pl.ds(LANES, extra)]
        move(weight.at[pl.ds(0, LANES)], sent.at[pl.ds(k * LANES, LANES)])
        move(last, sent.at[pl.ds(3 * LANES + k * extra, extra)])
        move(last, third.at[pl.ds(k * LANES, extra)])
    for k in range(3):
        third[k * LANES + extra : (k + 1) * LANES] = jnp.zeros((LANES - extra, third.shape[1]), BF16)
    table = [v[...].astype(F32).reshape(1, -1) for v in (g1, s1, g2, s2, ob, db, ub)]
    query_bias, value_bias = (v[...].astype(F32).reshape(1, -1) for v in (qb, vb))
    hole = jnp.zeros((1, LANES), F32)
    gap = jnp.zeros((1, LANES - extra), F32)
    ends = [jnp.concatenate([v[:, LANES:], gap], 1) for v in (query_bias, value_bias)]
    table.append(jnp.concatenate([query_bias[:, :LANES], hole, value_bias[:, :LANES], ends[0], hole, ends[1]], 1))
    table = jnp.concatenate(table, 0)
    params[...] = table
    sent[3 * LANES + 3 * extra :] = jnp.concatenate([table, table], 0).astype(BF16)
    for copy in copies:
        copy.wait()
    pick(up, lambda copy: copy.wait())


def first_body(s, n, tokens, params, pair_weight, third_weight, normed_out, pair_out, third_out):
    normal, _ = normalize(tokens[0].astype(F32))
    normed = (normal * params[0:1] + params[1:2]).astype(BF16)
    normed_out[...] = normed
    span = pair_weight.shape[0]
    pair_out[...] = scaled(dot(normed, pair_weight[...], NT) + params[7:8, :span])
    third_out[...] = scaled(dot(normed, third_weight[...], NT) + params[7:8, span:])


def head_view(ref, rows, start, head, heads):
    value = ref[rows, start : start + LANES]
    if heads == 1:
        return value
    lane = lax.broadcasted_iota(jnp.int32, (1, LANES), 1)
    keep = (lane < HEAD_DIM) if head == 0 else (lane >= HEAD_DIM)
    return jnp.where(keep, value, jnp.zeros((), BF16))


def pick_head(values):
    if len(values) == 1:
        return values[0]
    lane = lax.broadcasted_iota(jnp.int32, (1, LANES), 1)
    return jnp.where(lane < HEAD_DIM, values[0], values[1])


def attend_part(queries, sources, attended, logsum, limit, block):
    count = queries[0].shape[0] // block
    keys = [source[:limit, LANES : 2 * LANES] for source in sources]
    values = [source[:limit, 2 * LANES :] for source in sources]

    def scores(unit):
        at, head = unit
        rows = slice(at * block, (at + 1) * block)
        return dot(head_view(queries[head // 2], rows, 0, head, 2 - head // 2), keys[head // 2], NT)

    units = [(at, head) for at in range(count) for head in range(3)]
    current = scores(units[0])
    done = []
    for index, (at, head) in enumerate(units):
        following = scores(units[index + 1]) if index + 1 < len(units) else None
        peak = jnp.max(current, -1, keepdims=True)
        expo = jnp.exp2(current - peak)
        total = jnp.sum(expo, -1, keepdims=True)
        mixed = dot(expo.astype(BF16), values[head // 2], NN)
        done.append((mixed * (1.0 / total), jnp.broadcast_to(peak + jnp.log2(total), mixed.shape)))
        current = following
        if head == 2:
            rows = slice(at * block, (at + 1) * block)
            attended[rows, :LANES] = pick_head([done[0][0], done[1][0]]).astype(BF16)
            attended[rows, LANES:] = done[2][0].astype(BF16)
            table = jnp.transpose(pick_head([done[0][1], done[1][1]]))
            logsum[:8, rows] = jnp.concatenate([table[0:4], table[HEAD_DIM : HEAD_DIM + 4]], 0)
            logsum[8:, rows] = jnp.transpose(done[2][1])[:8]
            done = []


def attend_body(s, n, query_pair, query_third, pair, third, attended, logsum):
    full = pair.shape[0]

    @pl.when(n[s[0]] == full)
    def _():
        attend_part((query_pair, query_third), (pair, third), attended, logsum, full, BLOCK)

    @pl.when(n[s[0]] != full)
    def _():
        attend_part((query_pair, query_third), (pair, third), attended, logsum, SHORT, BLOCK)


def attend_back_part(qkv, grad, logsum, inner, grads, heads, limit, block, full):
    count = -(-limit // block)
    keys = qkv[:limit, LANES : 2 * LANES]
    values = qkv[:limit, 2 * LANES :]

    def span(at):
        return slice(at * block, min((at + 1) * block, limit))

    def front(unit):
        head, at = unit
        query = head_view(qkv, span(at), 0, head, heads)
        pull = head_view(grad, span(at), 0, head, heads)
        return dot(keys, query, NT), dot(values, pull, NT), query, pull

    def put(rows, start, head, value):
        value = value.astype(BF16)
        if head == 1:
            value = pick_head([grads[rows, start : start + LANES], value])
        grads[rows, start : start + LANES] = value

    units = [(head, at) for head in range(heads) for at in range(count)]
    current = front(units[0])
    for index, (head, at) in enumerate(units):
        following = front(units[index + 1]) if index + 1 < len(units) else None
        scores, grad_probs, query, pull = current
        at_row = slice(4 * head, 4 * head + 1)
        probs = jnp.exp2(scores - logsum[at_row, span(at)])
        grad_scores = (probs * (grad_probs - inner[at_row, span(at)])).astype(BF16)
        value_part = dot(probs.astype(BF16), pull, NN)
        key_part = dot(grad_scores, query, NN)
        grad_values = value_part if at == 0 else grad_values + value_part
        grad_keys = key_part if at == 0 else grad_keys + key_part
        put(span(at), 0, head, dot(grad_scores, keys, TN) * HEAD_DIM**-0.5)
        if at == count - 1:
            put(slice(0, limit), LANES, head, grad_keys * LN2)
            put(slice(0, limit), 2 * LANES, head, grad_values)
        current = following
    if limit < full:
        grads[limit:, :] = jnp.zeros((full - limit, grads.shape[1]), BF16)


def attend_back_body(heads, s, n, qkv, grad, logsum, inner, grads):
    full = qkv.shape[0]

    @pl.when(n[s[0]] == full)
    def _():
        attend_back_part(qkv, grad, logsum, inner, grads, heads, full, BLOCK, full)

    @pl.when(n[s[0]] != full)
    def _():
        attend_back_part(qkv, grad, logsum, inner, grads, heads, SHORT, BLOCK, full)


def middle_body(s, n, tokens, params, *refs):
    arrays, weights, (middle_out, normed_out) = refs[:4], refs[4:8], refs[8:]
    branch = params[4:5]
    for array, weight in zip(arrays, weights):
        branch = branch + dot(array[:, : weight.shape[0]], weight[...], NN)
    middle = tokens[0].astype(F32) + branch
    middle_out[...] = middle.astype(BF16)
    normal, _ = normalize(middle)
    normed_out[...] = (normal * params[2:3] + params[3:4]).astype(BF16)


def gelu_and_slope(values):
    t = 1.0 / (1.0 + (0.3275911 * 0.7071067811865476) * jnp.abs(values))
    series = t * (
        (0.5 * 0.254829592)
        + t * ((0.5 * -0.284496736) + t * ((0.5 * 1.421413741) + t * ((0.5 * -1.453152027) + t * (0.5 * 1.061405429))))
    )
    decay = jnp.exp2(values * values * (-0.5 * LOG2E))
    tail = series * decay
    share = jnp.where(values >= 0, 1.0 - tail, tail)
    return values * share, share + values * (decay * 0.3989422804014327)


def hidden_part(normed, grad_feed, up, down, bias, active_out, upper_out, bias_out, put):
    block = normed.shape[0]
    count = 1

    def front(at):
        rows = slice(at * block, (at + 1) * block)
        return dot(normed[rows], up[...], NN), dot(grad_feed[rows], down[...], NT)

    current = front(0)
    total = None
    for at in range(count):
        following = front(at + 1) if at + 1 < count else None
        rows = slice(at * block, (at + 1) * block)
        active, slope = gelu_and_slope(current[0] + bias)
        active = active.astype(BF16)
        active_out[rows] = active
        grad_upper = (current[1] * slope).astype(BF16)
        upper_out[rows] = grad_upper
        put(rows, dot(active, down[...], NN), dot(grad_upper, up[...], NT))
        sums = sum_rows(grad_upper)
        total = sums if total is None else total + sums
        current = following
    accumulate(bias_out, total)


def hidden_own_body(s, n, normed, cot, up, down, params, feed_grad_out, active_out, upper_out, feed_out, back_out, bias_out):
    position = pl.program_id(0) * ROWS + lax.broadcasted_iota(jnp.int32, (ROWS, 1), 0)
    grad_feed = jnp.where(position < n[s[0]], cot[0], jnp.zeros((), BF16))
    feed_grad_out[...] = grad_feed

    def put(rows, feed, back):
        feed_out[rows] = feed.astype(BF16)
        back_out[rows] = back.astype(BF16)

    hidden_part(normed[...], grad_feed, up, down, params[6:7], active_out, upper_out, bias_out, put)


def hidden_far_body(s, n, normed, grad_feed, feed_in, back_in, g0, g1, o0, o1, small, *refs):
    (active_out, upper_out, feed_out, back_out, bias_out), (up, down, sems) = refs[:5], refs[5:]
    part = g0.shape[0]

    @pl.when(pl.program_id(0) == 0)
    def _():
        def fill(first, second):
            copies = []
            for at, (target, sources) in enumerate(((up, first), (down, second))):
                rows = (pl.ds(0, part), pl.ds(part, target.shape[0] - part))
                for k, source in enumerate(sources):
                    copies.append(pltpu.make_async_copy(source, target.at[rows[k]], sems.at[2 * at + k]))
            for copy in copies:
                copy.start()
            for copy in copies:
                copy.wait()

        @pl.when(s[2] == 0)
        def _():
            fill((g0, g1), (o0, o1))

        @pl.when(s[2] != 0)
        def _():
            fill((o0, o1), (g0, g1))

    def put(rows, feed, back):
        feed_out[rows] = (feed_in[rows].astype(F32) + feed).astype(BF16)
        back_out[rows] = (back_in[rows].astype(F32) + back).astype(BF16)

    hidden_part(normed[...], grad_feed[...], up, down, small[6:7].astype(F32), active_out, upper_out, bias_out, put)


def output_body(s, n, middle, feed, side, params, own_out):
    total = feed[...].astype(F32) + side[...].astype(F32)
    own_out[...] = (middle[...].astype(F32) + total + params[5:6]).astype(BF16)


def split_body(s, n, whole_in, *outs):
    count = outs[0].shape[0]
    mine = 2 * s[4] + s[5]
    for k, out in enumerate(outs):
        start = pl.multiple_of((mine ^ k) * count, 8)
        out[...] = whole_in[pl.ds(start, count)]


def second_body(s, n, *refs):
    up, down = refs[:4], refs[4:8]
    outs = refs[8:]
    for (near, got_near, away, got_away), bit, (kept, sent) in ((up, s[5], outs[:2]), (down, s[4], outs[2:])):
        count = kept.shape[1]
        for k, (own, got) in enumerate(((near, got_near), (away, got_away))):
            for target, half in ((kept, bit), (sent, 1 - bit)):
                rows = pl.ds(pl.multiple_of(half * count, 8), count)
                target[k] = (own[rows].astype(F32) + got[rows].astype(F32)).astype(BF16)


def third_body(s, n, up, got_up, down, got_down, up_out, down_out, sent):
    count = up.shape[1]
    for k, (own, got, out) in enumerate(((up, got_up, up_out), (down, got_down, down_out))):
        out[...] = (own[0].astype(F32) + got[0].astype(F32)).astype(BF16)
        sent[k * count : (k + 1) * count] = (own[1].astype(F32) + got[1].astype(F32)).astype(BF16)


def join_hidden_body(s, n, up, up_near, up_other, down, down_near, down_other, up_out, down_out):
    count = up.shape[0]
    first, second = slice(0, count), slice(count, 2 * count)
    lists = (
        (up_out, s[4], s[5], ((0, 0, up, first), (0, 1, up_near, first), (1, 0, up_other, first), (1, 1, up_other, second))),
        (down_out, s[5], s[4], ((0, 0, down, first), (0, 1, down_near, first), (1, 0, down_other, first), (1, 1, down_other, second))),
    )
    for out, high, low, pieces in lists:
        for at_high, at_low, piece, rows in pieces:
            place = 2 * (high ^ at_high) + (low ^ at_low)
            out[pl.ds(pl.multiple_of(place * count, 8), count)] = piece[rows].astype(F32)


def join_mixed_body(s, n, *refs):
    pieces, (out, query, key, value), (pair, last) = refs[:4], refs[4:8], refs[8:]
    count = pieces[0].shape[0] // 2
    group, extra = out.shape[0], out.shape[0] - LANES
    for k, piece in enumerate(pieces):
        place = 2 * (s[4] ^ (k // 2)) + (s[5] ^ (k % 2))
        rows = pl.ds(pl.multiple_of(place * count, 8), count)
        pair[rows] = piece[:count].astype(F32)
        last[rows] = piece[count:].astype(F32)
    out[...] = last[:group]
    for k, target in enumerate((query, key, value)):
        target[:LANES] = pair[k * LANES : (k + 1) * LANES]
        target[LANES:] = last[group + k * extra : group + (k + 1) * extra]


def mix_body(s, n, pair, got_pair, p0, p1, p2, p3, out):
    count = got_pair.shape[0]
    out[:count] = (pair[...].astype(F32) + got_pair[...].astype(F32)).astype(BF16)
    total = (p0[...].astype(F32) + p1[...].astype(F32)) + (p2[...].astype(F32) + p3[...].astype(F32))
    out[count:] = total.astype(BF16)


def assemble_body(places, s, n, *refs):
    pieces, result, sems = refs[: len(places)], refs[-2], refs[-1]
    copies = []
    for k, ((where, start), piece) in enumerate(zip(places, pieces)):
        target = result.at[s[3] ^ where, pl.ds(start, piece.shape[0])]
        copies.append(pltpu.make_async_copy(piece, target, sems.at[k]))
        copies[-1].start()
    for copy in copies:
        copy.wait()


def back_two_body(s, n, middle, grad_feed, g0, g1, params, w0, w1, a0, a1, branch_out, *refs):
    grad_tiles, inner_outs, sums_out = refs[:4], refs[4:8], refs[8]
    normal, inverse = normalize(middle[...].astype(F32))
    grad_normed = g0[...].astype(F32) + g1[...].astype(F32)
    grad_output = grad_feed[...].astype(F32)
    grad_middle = grad_output + norm_back(grad_normed, normal, inverse, params[2:3])
    grad_branch = grad_middle.astype(BF16)
    branch_out[...] = grad_branch
    sums = jnp.concatenate(
        [
            column_sums(grad_normed * normal),
            column_sums(grad_normed),
            column_sums(grad_branch.astype(F32)),
            column_sums(grad_output),
        ],
        0,
    )
    accumulate(sums_out, sums)
    lane = lax.broadcasted_iota(jnp.int32, (8, LANES), 1)
    head = lax.broadcasted_iota(jnp.int32, (8, LANES), 0)
    member = (lane // HEAD_DIM == head // 4).astype(BF16)
    for k, (weight, array) in enumerate(((w0, a0), (w1, a1))):
        grad_att = dot(grad_branch, weight[...], NT).astype(BF16)
        extra = grad_att.shape[1] - LANES
        gap = jnp.zeros((grad_att.shape[0], LANES - extra), BF16)
        for t in range(2):
            lanes = slice(t * LANES, (t + 1) * LANES)
            part = grad_att[:, :LANES] if t == 0 else jnp.concatenate([grad_att[:, LANES:], gap], 1)
            grad_tiles[2 * k + t][...] = part
            product = part.astype(F32) * array[:, lanes].astype(F32)
            high = product.astype(BF16)
            low = (product - high.astype(F32)).astype(BF16)
            inner_outs[2 * k + t][...] = dot(member, high, NT) + dot(member, low, NT)


def back_one_body(s, n, tokens, grad_middle, g0, g1, g2, g3, params, own_out, sums_out):
    normal, inverse = normalize(tokens[0].astype(F32))
    grad_normed = (g0[...].astype(F32) + g1[...].astype(F32)) + (g2[...].astype(F32) + g3[...].astype(F32))
    accumulate(
        sums_out, jnp.concatenate([column_sums(grad_normed * normal), column_sums(grad_normed)], 0)
    )
    back = norm_back(grad_normed, normal, inverse, params[0:1])
    own_out[...] = (grad_middle[...].astype(F32) + back).astype(BF16)


def pairs(count, mask):
    return [(i, i ^ mask) for i in range(count)]


def overlap(moves, kernel=None, inputs=()):
    operands, inputs = lax.optimization_barrier((tuple(v for _, v in moves), tuple(inputs)))
    received = tuple(move(v) for (move, _), v in zip(moves, operands))
    results = tuple(kernel(*inputs)) if kernel else ()
    return lax.optimization_barrier((received, results))


def after(value, *others):
    return lax.optimization_barrier((value, *others))[0]


def local(
    dp, tp,
    tokens, cube_lengths, query_weight, query_bias, key_weight, value_weight, value_bias,
    out_weight, out_bias, first_gain, first_shift, second_gain, second_shift,
    up_weight, up_bias, down_weight, down_bias, cotangent,
):
    slots, length, width = tokens.shape
    group = query_weight.shape[1]
    hidden = up_weight.shape[1]
    blocks = length // ROWS
    half = length // 2
    half_rows = half // 2
    mine = lax.axis_index("tp")
    place = lax.axis_index("dp")
    cube, core = mine // 2, mine % 2
    parity = place & 1
    bits = [1 << k for k in range(dp.bit_length() - 1)]
    scalars = (jnp.stack([cube, core, parity, mine, parity, (place // 2) & 1]).astype(jnp.int32), cube_lengths)

    def to_core(v):
        return lax.ppermute(v, "tp", pairs(tp, 1))

    def to_chip(v):
        return lax.ppermute(v, "tp", pairs(tp, 2))

    def to_place(v, mask):
        return lax.ppermute(v, "dp", pairs(dp, mask))

    full = (length, width)
    span = 3 * LANES
    extra = group - LANES
    vectors = whole((8, width))
    part_spec = whole((span, width))
    part_shape = shape_of((length, span), BF16)

    top = span + 3 * extra
    far_shape = (top + 16, width)
    anywhere = pl.BlockSpec(memory_space=pl.ANY)
    vector = pl.BlockSpec((width,), lambda i, s, n: (0,))
    short_vector = pl.BlockSpec((group,), lambda i, s, n: (0,))
    lead_rows = (2 * hidden // 3) // LANES * LANES
    sent, third_0, params, lead, rest = run(
        pack_body, scalars, (1,),
        [anywhere] * 5 + [vector] * 7 + [short_vector] * 2,
        [whole(far_shape), part_spec, vectors, whole((lead_rows, width)), whole((hidden - lead_rows, width))],
        [shape_of(far_shape, BF16), shape_of((span, width), BF16), shape_of((8, width), F32),
         shape_of((lead_rows, width), BF16), shape_of((hidden - lead_rows, width), BF16)],
        scratch=[pltpu.SemaphoreType.DMA((12,))],
        name="pack_weights", room=10,
    )(
        *map(in_hbm, (
            query_weight.T, key_weight.T, value_weight.T, up_weight, down_weight,
            first_gain, first_shift, second_gain, second_shift, out_bias, down_bias, up_bias, query_bias, value_bias,
        ))
    )
    far = to_chip(sent)

    def spread(rows):
        gap = ((0, 0), (0, LANES - extra), (0, 0))
        return jnp.pad(rows.reshape(3, extra, width), gap).reshape(span, width)

    normed, part_0, part_1 = run(
        first_body, scalars, (blocks,),
        [cube_rows(width), vectors, part_spec, part_spec],
        [rows_of(width), rows_of(span), rows_of(span)],
        [shape_of(full, BF16), part_shape, part_shape],
        name="first_norm_project", room=10,
    )(in_hbm(tokens), params, sent, third_0)
    pair_0 = sent[:span]

    def attend(pair, third):
        step = length // 2
        query = pl.BlockSpec((step, LANES), lambda i, s, n: (i, 0))
        return run(
            attend_body, scalars, (2,),
            [query, query, whole((length, span)), whole((length, span))],
            [pl.BlockSpec((step, 2 * LANES), lambda i, s, n: (i, 0)), pl.BlockSpec((16, step), lambda i, s, n: (0, i))],
            [shape_of((length, 2 * LANES), BF16), shape_of((16, length), F32)],
            name="attend", room=14,
        )(pair, third, pair, third)

    def project(weight, bias, at):
        return scaled(dot(normed, weight, NT) + bias[:, at * span : (at + 1) * span])

    att_0, log_0 = attend(part_0, part_1)
    far = after(far, att_0)
    pair_1, third_1 = far[:span], spread(far[span:top])
    bias_1 = far[top + 7 : top + 8].astype(F32)
    part_2 = project(pair_1, bias_1, 0)
    part_3 = project(third_1, bias_1, 1)
    got_0 = to_chip(after(lead, far))
    (side_0, out_far), (att_1, log_1) = overlap([(to_core, att_0), (to_chip, out_weight)], attend, (part_2, part_3))
    out_side = to_core(jnp.concatenate([out_weight, out_far], 0))
    side_1 = to_core(att_1)

    double_tile = rows_of(2 * LANES)

    def out_block(at):
        return pl.BlockSpec((group, width), lambda i, s, n: (at, 0))

    out_specs = [out_block(0), out_block(0), out_block(0), out_block(1)]
    middle, normed_two = run(
        middle_body, scalars, (blocks,),
        [cube_rows(width), vectors] + [double_tile] * 4 + out_specs,
        [rows_of(width)] * 2,
        [hbm_shape(full, BF16), shape_of(full, BF16)],
        name="attention_out_norm", room=12,
    )(in_hbm(tokens), params, att_0, att_1, side_0, side_1, out_weight, out_far, out_side, out_side)

    own_spec = pl.BlockSpec((half_rows, width), lambda i, s, n: (s[1] * 2 + i, 0))
    plain = pl.BlockSpec((half_rows, width), lambda i, s, n: (i, 0))
    own_shape = shape_of((half, width), BF16)

    def assemble(pieces, base=None):
        bases = [] if base is None else [base]
        return run(
            partial(assemble_body, tuple(place for place, _ in pieces)), scalars, (1,),
            [whole(piece.shape) for _, piece in pieces] + [anywhere] * len(bases), [anywhere], [shape_of((tp, half, width), BF16)],
            scratch=[pltpu.SemaphoreType.DMA((len(pieces),))], alias={len(pieces): 0} if bases else None,
            name="assemble", room=12,
        )(*(piece for _, piece in pieces), *bases)[0]

    def side_half(v):
        return lax.dynamic_slice(v, ((1 - core) * half, 0), (half, v.shape[1]))

    def bit_of(mask):
        return (place // mask) & 1

    def half_at(v, bit):
        count = v.shape[-2] // 2
        return lax.dynamic_slice_in_dim(v, bit * count, count, v.ndim - 2)

    def half_out(v, mask):
        return half_at(v, 1 - bit_of(mask))

    def half_kept(v, mask):
        return half_at(v, bit_of(mask))

    def add(a, b):
        return (a.astype(F32) + b.astype(F32)).astype(BF16)

    def join(v, other, mask):
        return jnp.where(bit_of(mask) == 0, jnp.concatenate([v, other], 0), jnp.concatenate([other, v], 0))

    both = shape_of((length, hidden), BF16)
    hidden_shapes = [both, both, hbm_shape(full, BF16), shape_of(full, BF16), shape_of((1, hidden), F32)]

    hidden_specs = [rows_of(hidden), rows_of(hidden), rows_of(width), rows_of(width), whole((1, hidden))]

    own_call = run(
        hidden_own_body, scalars, (blocks,),
        [rows_of(width), cube_rows(width), whole((width, hidden)), whole((hidden, width)), vectors],
        [rows_of(width)] + hidden_specs,
        [shape_of(full, BF16)] + hidden_shapes,
        name="hidden_own", room=16,
    )
    (got_1, other_0), (grad_feed, active_0, upper_0, feed, back, up_bias_0) = overlap(
        [(to_chip, rest), (partial(to_place, mask=1), got_0)],
        own_call,
        (normed_two, in_hbm(cotangent), in_hbm(up_weight), in_hbm(down_weight), params),
    )
    other_1 = to_place(got_1, 1)

    def hidden_grads(active, upper):
        return dot(normed_two, upper, TN).astype(BF16), dot(active, grad_feed, TN).astype(BF16)

    near = hidden_grads(active_0, upper_0)
    orders = [bits, bits[1:2] + bits[:1] + bits[2:]]
    far_call = run(
        hidden_far_body, scalars, (blocks,),
        [rows_of(width)] * 4 + [anywhere] * 4 + [pl.BlockSpec((16, width), lambda i, s, n: (top // 16, 0))],
        hidden_specs,
        [hbm_shape(both.shape, BF16)] * 2 + hidden_shapes[2:],
        scratch=[pltpu.VMEM((width, hidden), BF16), pltpu.VMEM((hidden, width), BF16), pltpu.SemaphoreType.DMA((4,))],
        name="hidden_far", room=16,
    )

    square = [bits[1], bits[0], bits[0] | bits[1]]

    def quarters(v):
        piece = (v.shape[0] // 4, v.shape[1])
        return run(
            split_body, scalars, (1,), [whole(v.shape)], [whole(piece)] * 4, [shape_of(piece, BF16)] * 4, name="split", room=8
        )(v)

    def to_square(pieces):
        return [(partial(to_place, mask=mask), v) for mask, v in zip(square, pieces)]

    sent_near = [half_out(v, order[0]) for v, order in zip(near, orders)]

    def over(order, k):
        return lambda v: to_place(v, order[k])

    got_near, (active_1, upper_1, feed, back, up_bias_1) = overlap(
        [(over(order, 0), v) for v, order in zip(sent_near, orders)],
        far_call,
        (normed_two, grad_feed, feed, back, got_0, got_1, other_0, other_1, far),
    )
    side_back = to_core(back)
    side_feed = to_core(side_half(feed))
    away = hidden_grads(active_1, upper_1)
    (own_output,) = run(
        output_body, scalars, (2,),
        [own_spec] * 2 + [plain, vectors],
        [plain], [own_shape], name="output", room=8,
    )(after(middle, *away), feed, side_feed, params)
    sent_away = [half_out(v, order[0]) for v, order in zip(away, orders)]

    tile = rows_of(LANES)
    tile_shape = hbm_shape((length, LANES), BF16)
    inner_shape = hbm_shape((8, length), F32)
    two_call = run(
        back_two_body, scalars, (blocks,),
        [rows_of(width)] * 4 + [vectors] + out_specs[:2] + [double_tile] * 2,
        [rows_of(width)] + [tile] * 4 + [pl.BlockSpec((8, ROWS), lambda i, s, n: (0, i))] * 4 + [whole((4, width))],
        [hbm_shape(full, BF16)] + [tile_shape] * 4 + [inner_shape] * 4 + [shape_of((4, width), F32)],
        name="second_norm_back", room=13,
    )
    (far_output_0, side_output, *got_away), results = overlap(
        [(to_chip, own_output[:half_rows]), (to_core, own_output)] + [(over(order, 0), v) for v, order in zip(sent_away, orders)],
        two_call,
        (middle, in_hbm(grad_feed), back, side_back, params, out_weight, out_far, in_hbm(att_0), in_hbm(att_1)),
    )
    grad_branch, gt_0, gt_1, gt_2, gt_3, in_0, in_1, in_2, in_3, sums_two = results

    def attend_back(qkv, grad, logsum, inner, count):
        at = 2 - count
        return run(
            partial(attend_back_body, count), scalars, (1,),
            [whole((length, span)), whole((length, LANES)), pl.BlockSpec((8, length), lambda i, s, n: (at, 0)), whole((8, length))],
            [whole((length, span))],
            [part_shape],
            name="attend_back", room=13,
        )(qkv, grad, logsum, inner)

    def weight_grad(grads):
        return dot(grads, normed, TN).astype(BF16)

    def third_only(v):
        return v.reshape(3, LANES, width)[:, :extra].reshape(3 * extra, width)

    pair_back, third_back = partial(attend_back, count=2), partial(attend_back, count=1)
    second_half = hidden // 2
    kept_rows = [pl.BlockSpec((second_half, width), lambda i, s, n: (s[4], 0)), pl.BlockSpec((second_half, width), lambda i, s, n: (s[5], 0))]
    piece = whole((second_half, width))
    two_shape = (2, second_half // 2, width)
    up_kept, up_sent, down_kept, down_sent = run(
        second_body, scalars, (1,),
        [kept_rows[0], piece, kept_rows[0], piece, kept_rows[1], piece, kept_rows[1], piece],
        [whole(two_shape)] * 4, [shape_of(two_shape, BF16)] * 4, name="second_halving", room=12,
    )(near[0], got_near[0], away[0], got_away[0], near[1], got_near[1], away[1], got_away[1])
    sent_2 = [up_sent, down_sent]
    (far_output_1, across_output_0, *got_second), (grads_2,) = overlap(
        [(to_chip, own_output[half_rows:]), (to_core, far_output_0)] + [(over(order, 1), v) for v, order in zip(sent_2, orders)],
        pair_back,
        (part_2, gt_2, log_1, in_2),
    )
    quarter_shape = (second_half // 2, width)
    up_third, down_third, sent_3 = run(
        third_body, scalars, (1,),
        [whole(two_shape)] * 4, [whole(quarter_shape)] * 2 + [piece],
        [shape_of(quarter_shape, BF16)] * 2 + [shape_of((second_half, width), BF16)], name="third_sum", room=10,
    )(up_kept, got_second[0], down_kept, got_second[1])
    (across_output_1, got_third), (grads_0,) = overlap(
        [(to_core, far_output_1), (to_chip, sent_3)], pair_back, (part_0, gt_0, log_0, in_0)
    )
    out_grads = [dot(a, grad_branch, TN).astype(BF16)[:group] for a in (att_0, att_1)]
    quarter = got_third.shape[0] // 2
    stage_4 = [add(v, got_third[k * quarter : (k + 1) * quarter]) for k, v in enumerate((up_third, down_third))]
    pair_away = weight_grad(grads_2)
    back_most = dot(grads_2, pair_1, NN) + dot(grads_0, pair_0, NN)
    (pair_far, got_up), (grads_3,) = overlap(
        [(to_chip, pair_away), (over(bits, 2), stage_4[0])], third_back, (part_3, gt_3, log_1, in_3)
    )
    third_away = third_only(weight_grad(grads_3))
    back_most = (back_most + dot(grads_3, third_1, NN)).astype(BF16)
    side_most_sent = side_half(back_most)
    pair = add(weight_grad(grads_0), pair_far)
    sent_pair = half_out(pair, bits[0])
    last_away = jnp.concatenate([out_grads[1], third_away], 0)
    (got_pair, last_far, side_most, got_down), (grads_1,) = overlap(
        [(over(bits, 0), sent_pair), (to_chip, last_away), (to_core, side_most_sent), (over(bits, 2), stage_4[1])],
        third_back,
        (part_1, gt_1, log_0, in_1),
    )
    back_last = dot(grads_1, third_0, NN).astype(BF16)
    side_last = to_core(side_half(back_last))
    last = add(jnp.concatenate([out_grads[0], third_only(weight_grad(grads_1))], 0), last_far)
    last_pieces = quarters(last)
    pair = add(half_kept(pair, bits[0]), got_pair)
    sent_pair = half_out(pair, bits[1])
    totals = [add(v, g) for v, g in zip(stage_4, (got_up, got_down))]
    for mask in bits[3:]:
        totals = [add(v, to_place(v, mask)) for v in totals]

    token_spec = pl.BlockSpec((1, half_rows, width), lambda i, s, n: (s[0], s[1] * 2 + i, 0))
    one_call = run(
        back_one_body, scalars, (2,),
        [token_spec, own_spec, own_spec, own_spec, plain, plain, vectors],
        [plain, whole((2, width))],
        [own_shape, shape_of((2, width), F32)],
        name="first_norm_back", room=14,
    )
    (got_pair, *got_last), (own_grad, sums_one) = overlap(
        [(over(bits, 1), sent_pair)] + to_square(last_pieces[1:]),
        one_call,
        (in_hbm(tokens), in_hbm(grad_branch), back_most, back_last, side_most, side_last, params),
    )

    first_part = half // 3 // LANES * LANES
    def beside_first(own, side, far_0, far_1, across_0, across_1, *parts):
        whole_output = assemble([
            ((0, 0), own), ((1, 0), side), ((2, 0), far_0), ((2, half_rows), far_1), ((3, 0), across_0), ((3, half_rows), across_1),
        ])
        count = parts[1].shape[0]
        (mixed,) = run(
            mix_body, scalars, (1,),
            [pl.BlockSpec((count, width), lambda i, s, n: (s[5], 0))] + [whole(v.shape) for v in parts[1:]],
            [whole((2 * count, width))], [shape_of((2 * count, width), BF16)], name="mix", room=8,
        )(*parts)
        return whole_output, mixed

    (far_0, side_grad, up_near, down_near, first_sums), (output, mixed) = overlap(
        [(to_chip, own_grad[:first_part]), (to_core, own_grad)]
        + [(over(order, 1), v) for v, order in zip(totals, orders)]
        + [(to_core, sums_one)],
        beside_first,
        (own_output, side_output, far_output_0, far_output_1, across_output_0, across_output_1, pair, got_pair, last_pieces[0], *got_last),
    )
    output = output.reshape(slots, length, width)
    first_sums = sums_one + first_sums

    def bias_sums(pair, third):
        return jnp.concatenate([sum_rows(pair), sum_rows(third)], 1)

    shared = [sums_two, first_sums]
    sums = jnp.concatenate(shared + [up_bias_0, bias_sums(grads_0, grads_1)], 0)
    sums_away = jnp.concatenate(shared + [up_bias_1, bias_sums(grads_2, grads_3)], 0)
    both_up, both_down = (jnp.concatenate([v, g], 0) for v, g in zip(totals, (up_near, down_near)))
    (far_1, up_other, down_other, got_mixed, got_sums), _ = overlap(
        [(to_chip, own_grad[first_part:]), (over(bits, 0), both_up), (over(bits, 1), both_down), (over(bits, 2), mixed), (to_chip, sums_away)]
    )
    mixed = add(mixed, got_mixed)
    for mask in bits[3:]:
        mixed = add(mixed, to_place(mixed, mask))
    sums = sums + got_sums

    def beside_last(own, side, far_0, far_1, *parts):
        base = assemble([((0, 0), own), ((1, 0), side), ((2, 0), far_0), ((2, first_part), far_1)])
        shape = (hidden, width)
        hidden_grads = run(
            join_hidden_body, scalars, (1,), [whole(v.shape) for v in parts], [whole(shape)] * 2, [shape_of(shape, F32)] * 2,
            name="join_hidden", room=14,
        )(*parts)
        return base, *hidden_grads

    (*got_mixed, across_1, across_0), (base, up_total, down_total) = overlap(
        to_square([mixed] * 3) + [(to_core, far_1), (to_core, far_0)],
        beside_last,
        (own_grad, side_grad, far_0, far_1, totals[0], up_near, up_other, totals[1], down_near, down_other),
    )
    got_z, got_y, got_yz = overlap(to_square([sums] * 3))[0]
    sums = (sums + got_y) + (got_z + got_yz)
    for mask in bits[2:]:
        sums = sums + to_place(sums, mask)
    out_grad, *qkv_grads = run(
        join_mixed_body, scalars, (1,), [whole(mixed.shape)] * 4, [whole((group, width))] * 4, [shape_of((group, width), F32)] * 4,
        scratch=[pltpu.VMEM((2 * group, width), F32)] * 2, name="join_mixed", room=12,
    )(mixed, *got_mixed)
    input_grad = assemble([((3, 0), across_0), ((3, first_part), across_1)], base).reshape(slots, length, width)

    def bias_of(k):
        start = k * LANES
        return jnp.concatenate([sums[7, start : start + LANES], sums[7, span + start : span + start + extra]])

    return (
        output,
        input_grad,
        qkv_grads[0].T,
        bias_of(0),
        qkv_grads[1].T,
        qkv_grads[2].T,
        bias_of(2),
        out_grad,
        sums[2],
        sums[4],
        sums[5],
        sums[0],
        sums[1],
        up_total,
        sums[6],
        down_total,
        sums[3],
    )


def solution(mesh):
    dp, tp = mesh.shape["dp"], mesh.shape["tp"]
    placed = (
        P("dp", None, None),
        P("dp"),
        P(None, "tp"),
        P("tp"),
        P(None, "tp"),
        P(None, "tp"),
        P("tp"),
        P("tp", None),
        P(),
        P(),
        P(),
        P(),
        P(),
        P(None, "tp"),
        P("tp"),
        P("tp", None),
        P(),
        P("dp", None, None),
    )
    return jax.shard_map(
        partial(local, dp, tp),
        mesh=mesh,
        in_specs=placed,
        out_specs=(
            P("dp", None, None),
            P("dp", None, None),
            P(None, "tp"),
            P("tp"),
            P(None, "tp"),
            P(None, "tp"),
            P("tp"),
            P("tp", None),
            P(),
            P(),
            P(),
            P(),
            P(),
            P(None, "tp"),
            P("tp"),
            P("tp", None),
            P(),
        ),
        check_vma=False,
    )
```

```python
from functools import partial

import jax
import jax.numpy as jnp
from jax import lax
from jax.experimental import pallas as pl
from jax.experimental.pallas import tpu as pltpu
from jax.sharding import PartitionSpec as P

HEAD_DIM = 64
SHORT = 864
ROWS = 384
BLOCK = 256
LANES = 128
WIDE = 256
EPS = 1e-06
LOG2E = 1.4426950408889634
LN2 = 0.6931471805599453
BF16 = jnp.bfloat16
F32 = jnp.float32

NN = (((1,), (0,)), ((), ()))
NT = (((1,), (1,)), ((), ()))
TN = (((0,), (0,)), ((), ()))


def dot(left, right, dims):
    return lax.dot_general(left, right, dims, preferred_element_type=F32)


def shape_of(shape, dtype):
    return jax.ShapeDtypeStruct(shape, dtype)


def hbm_shape(shape, dtype):
    return pltpu.HBM(shape, dtype)


def run(body, scalars, grid, in_specs, out_specs, out_shape, scratch=(), alias=None, name=None, room=20):
    def call(*arrays):
        return pl.pallas_call(
            body,
            grid_spec=pltpu.PrefetchScalarGridSpec(
                num_scalar_prefetch=2,
                grid=grid,
                in_specs=in_specs,
                out_specs=out_specs,
                scratch_shapes=list(scratch),
            ),
            out_shape=out_shape,
            input_output_aliases={k + 2: v for k, v in (alias or {}).items()},
            compiler_params=pltpu.CompilerParams(vmem_limit_bytes=room << 20),
            cost_estimate=pl.CostEstimate(flops=1000, transcendentals=0, bytes_accessed=1000),
            name=name,
        )(*scalars, *arrays)

    return call


def in_hbm(v):
    return pltpu.with_memory_space_constraint(v, pltpu.HBM)


def whole(shape):
    return pl.BlockSpec(shape, lambda i, s, n: (0,) * len(shape))


def rows_of(width, at=0):
    return pl.BlockSpec((ROWS, width), lambda i, s, n: (i, at))


def cube_rows(width):
    return pl.BlockSpec((1, ROWS, width), lambda i, s, n: (s[0], i, 0))


def normalize(values):
    center = values - jnp.mean(values, -1, keepdims=True)
    inverse = lax.rsqrt(jnp.mean(center * center, -1, keepdims=True) + EPS)
    return center * inverse, inverse


def norm_back(grad, normal, inverse, gain):
    scaled = grad * gain
    return inverse * (
        scaled
        - jnp.mean(scaled, -1, keepdims=True)
        - normal * jnp.mean(scaled * normal, -1, keepdims=True)
    )


def column_sums(values):
    return jnp.sum(values, 0, keepdims=True)


def sum_rows(values):
    return dot(jnp.ones((8, values.shape[0]), BF16), values, NN)[0:1]


def accumulate(ref, value):
    first = pl.program_id(0) == 0

    @pl.when(first)
    def _():
        ref[...] = value

    @pl.when(jnp.logical_not(first))
    def _():
        ref[...] += value


SCALE = HEAD_DIM**-0.5 * LOG2E


def scaled(part):
    lane = lax.broadcasted_iota(jnp.int32, (1, part.shape[1]), 1)
    return (part * jnp.where(lane < LANES, SCALE, 1.0)).astype(BF16)


def pack_body(s, n, query, key, value, up, down, g1, s1, g2, s2, ob, db, ub, qb, vb, sent, third, params, lead, rest, sems):
    extra = query.shape[0] - LANES
    copies = []

    def move(source, target):
        copies.append(pltpu.make_async_copy(source, target, sems.at[len(copies)]))
        copies[-1].start()

    def pick(weight, act):
        count = lead.shape[0]
        for k, (start, target) in enumerate(((0, lead), (count, rest))):
            act(pltpu.make_async_copy(weight.at[pl.ds(start, target.shape[0])], target, sems.at[10 + k]))

    @pl.when(s[2] == 0)
    def _():
        pick(up, lambda copy: copy.start())

    @pl.when(s[2] != 0)
    def _():
        pick(down, lambda copy: copy.start())

    for k, weight in enumerate((query, key, value)):
        last = weight.at[pl.ds(LANES, extra)]
        move(weight.at[pl.ds(0, LANES)], sent.at[pl.ds(k * LANES, LANES)])
        move(last, sent.at[pl.ds(3 * LANES + k * extra, extra)])
        move(last, third.at[pl.ds(k * LANES, extra)])
    for k in range(3):
        third[k * LANES + extra : (k + 1) * LANES] = jnp.zeros((LANES - extra, third.shape[1]), BF16)
    table = [v[...].astype(F32).reshape(1, -1) for v in (g1, s1, g2, s2, ob, db, ub)]
    query_bias, value_bias = (v[...].astype(F32).reshape(1, -1) for v in (qb, vb))
    hole = jnp.zeros((1, LANES), F32)
    gap = jnp.zeros((1, LANES - extra), F32)
    ends = [jnp.concatenate([v[:, LANES:], gap], 1) for v in (query_bias, value_bias)]
    table.append(jnp.concatenate([query_bias[:, :LANES], hole, value_bias[:, :LANES], ends[0], hole, ends[1]], 1))
    table = jnp.concatenate(table, 0)
    params[...] = table
    sent[3 * LANES + 3 * extra :] = jnp.concatenate([table, table], 0).astype(BF16)
    for copy in copies:
        copy.wait()
    pick(up, lambda copy: copy.wait())


def first_body(s, n, tokens, params, pair_weight, third_weight, normed_out, pair_out, third_out):
    normal, _ = normalize(tokens[0].astype(F32))
    normed = (normal * params[0:1] + params[1:2]).astype(BF16)
    normed_out[...] = normed
    span = pair_weight.shape[0]
    pair_out[...] = scaled(dot(normed, pair_weight[...], NT) + params[7:8, :span])
    third_out[...] = scaled(dot(normed, third_weight[...], NT) + params[7:8, span:])


def head_view(ref, rows, start, head, heads):
    value = ref[rows, start : start + LANES]
    if heads == 1:
        return value
    lane = lax.broadcasted_iota(jnp.int32, (1, LANES), 1)
    keep = (lane < HEAD_DIM) if head == 0 else (lane >= HEAD_DIM)
    return jnp.where(keep, value, jnp.zeros((), BF16))


def pick_head(values):
    if len(values) == 1:
        return values[0]
    lane = lax.broadcasted_iota(jnp.int32, (1, LANES), 1)
    return jnp.where(lane < HEAD_DIM, values[0], values[1])


def attend_part(queries, sources, attended, logsum, limit, block):
    count = queries[0].shape[0] // block
    keys = [source[:limit, LANES : 2 * LANES] for source in sources]
    values = [source[:limit, 2 * LANES :] for source in sources]

    def scores(unit):
        at, head = unit
        rows = slice(at * block, (at + 1) * block)
        return dot(head_view(queries[head // 2], rows, 0, head, 2 - head // 2), keys[head // 2], NT)

    units = [(at, head) for at in range(count) for head in range(3)]
    current = scores(units[0])
    done = []
    for index, (at, head) in enumerate(units):
        following = scores(units[index + 1]) if index + 1 < len(units) else None
        peak = jnp.max(current, -1, keepdims=True)
        expo = jnp.exp2(current - peak)
        total = jnp.sum(expo, -1, keepdims=True)
        mixed = dot(expo.astype(BF16), values[head // 2], NN)
        done.append((mixed * (1.0 / total), jnp.broadcast_to(peak + jnp.log2(total), mixed.shape)))
        current = following
        if head == 2:
            rows = slice(at * block, (at + 1) * block)
            attended[rows, :LANES] = pick_head([done[0][0], done[1][0]]).astype(BF16)
            attended[rows, LANES:] = done[2][0].astype(BF16)
            table = jnp.transpose(pick_head([done[0][1], done[1][1]]))
            logsum[:8, rows] = jnp.concatenate([table[0:4], table[HEAD_DIM : HEAD_DIM + 4]], 0)
            logsum[8:, rows] = jnp.transpose(done[2][1])[:8]
            done = []


def attend_body(s, n, query_pair, query_third, pair, third, attended, logsum):
    full = pair.shape[0]

    @pl.when(n[s[0]] == full)
    def _():
        attend_part((query_pair, query_third), (pair, third), attended, logsum, full, BLOCK)

    @pl.when(n[s[0]] != full)
    def _():
        attend_part((query_pair, query_third), (pair, third), attended, logsum, SHORT, BLOCK)


def attend_back_part(qkv, grad, logsum, inner, grads, heads, limit, block, full):
    count = -(-limit // block)
    keys = qkv[:limit, LANES : 2 * LANES]
    values = qkv[:limit, 2 * LANES :]

    def span(at):
        return slice(at * block, min((at + 1) * block, limit))

    def front(unit):
        head, at = unit
        query = head_view(qkv, span(at), 0, head, heads)
        pull = head_view(grad, span(at), 0, head, heads)
        return dot(keys, query, NT), dot(values, pull, NT), query, pull

    def put(rows, start, head, value):
        value = value.astype(BF16)
        if head == 1:
            value = pick_head([grads[rows, start : start + LANES], value])
        grads[rows, start : start + LANES] = value

    units = [(head, at) for head in range(heads) for at in range(count)]
    current = front(units[0])
    for index, (head, at) in enumerate(units):
        following = front(units[index + 1]) if index + 1 < len(units) else None
        scores, grad_probs, query, pull = current
        at_row = slice(4 * head, 4 * head + 1)
        probs = jnp.exp2(scores - logsum[at_row, span(at)])
        grad_scores = (probs * (grad_probs - inner[at_row, span(at)])).astype(BF16)
        value_part = dot(probs.astype(BF16), pull, NN)
        key_part = dot(grad_scores, query, NN)
        grad_values = value_part if at == 0 else grad_values + value_part
        grad_keys = key_part if at == 0 else grad_keys + key_part
        put(span(at), 0, head, dot(grad_scores, keys, TN) * HEAD_DIM**-0.5)
        if at == count - 1:
            put(slice(0, limit), LANES, head, grad_keys * LN2)
            put(slice(0, limit), 2 * LANES, head, grad_values)
        current = following
    if limit < full:
        grads[limit:, :] = jnp.zeros((full - limit, grads.shape[1]), BF16)


def attend_back_body(heads, s, n, qkv, grad, logsum, inner, grads):
    full = qkv.shape[0]

    @pl.when(n[s[0]] == full)
    def _():
        attend_back_part(qkv, grad, logsum, inner, grads, heads, full, BLOCK, full)

    @pl.when(n[s[0]] != full)
    def _():
        attend_back_part(qkv, grad, logsum, inner, grads, heads, SHORT, BLOCK, full)


def middle_body(s, n, tokens, params, *refs):
    arrays, weights, (middle_out, normed_out) = refs[:4], refs[4:8], refs[8:]
    branch = params[4:5]
    for array, weight in zip(arrays, weights):
        branch = branch + dot(array[:, : weight.shape[0]], weight[...], NN)
    middle = tokens[0].astype(F32) + branch
    middle_out[...] = middle.astype(BF16)
    normal, _ = normalize(middle)
    normed_out[...] = (normal * params[2:3] + params[3:4]).astype(BF16)


def gelu_and_slope(values):
    t = 1.0 / (1.0 + (0.3275911 * 0.7071067811865476) * jnp.abs(values))
    series = t * (
        (0.5 * 0.254829592)
        + t * ((0.5 * -0.284496736) + t * ((0.5 * 1.421413741) + t * ((0.5 * -1.453152027) + t * (0.5 * 1.061405429))))
    )
    decay = jnp.exp2(values * values * (-0.5 * LOG2E))
    tail = series * decay
    share = jnp.where(values >= 0, 1.0 - tail, tail)
    return values * share, share + values * (decay * 0.3989422804014327)


def hidden_part(normed, grad_feed, up, down, bias, active_out, upper_out, bias_out, put):
    block = normed.shape[0]
    count = 1

    def front(at):
        rows = slice(at * block, (at + 1) * block)
        return dot(normed[rows], up[...], NN), dot(grad_feed[rows], down[...], NT)

    current = front(0)
    total = None
    for at in range(count):
        following = front(at + 1) if at + 1 < count else None
        rows = slice(at * block, (at + 1) * block)
        active, slope = gelu_and_slope(current[0] + bias)
        active = active.astype(BF16)
        active_out[rows] = active
        grad_upper = (current[1] * slope).astype(BF16)
        upper_out[rows] = grad_upper
        put(rows, dot(active, down[...], NN), dot(grad_upper, up[...], NT))
        sums = sum_rows(grad_upper)
        total = sums if total is None else total + sums
        current = following
    accumulate(bias_out, total)


def hidden_own_body(s, n, normed, cot, up, down, params, feed_grad_out, active_out, upper_out, feed_out, back_out, bias_out):
    position = pl.program_id(0) * ROWS + lax.broadcasted_iota(jnp.int32, (ROWS, 1), 0)
    grad_feed = jnp.where(position < n[s[0]], cot[0], jnp.zeros((), BF16))
    feed_grad_out[...] = grad_feed

    def put(rows, feed, back):
        feed_out[rows] = feed.astype(BF16)
        back_out[rows] = back.astype(BF16)

    hidden_part(normed[...], grad_feed, up, down, params[6:7], active_out, upper_out, bias_out, put)


def hidden_far_body(s, n, normed, grad_feed, feed_in, back_in, g0, g1, o0, o1, small, *refs):
    (active_out, upper_out, feed_out, back_out, bias_out), (up, down, sems) = refs[:5], refs[5:]
    part = g0.shape[0]

    @pl.when(pl.program_id(0) == 0)
    def _():
        def fill(first, second):
            copies = []
            for at, (target, sources) in enumerate(((up, first), (down, second))):
                rows = (pl.ds(0, part), pl.ds(part, target.shape[0] - part))
                for k, source in enumerate(sources):
                    copies.append(pltpu.make_async_copy(source, target.at[rows[k]], sems.at[2 * at + k]))
            for copy in copies:
                copy.start()
            for copy in copies:
                copy.wait()

        @pl.when(s[2] == 0)
        def _():
            fill((g0, g1), (o0, o1))

        @pl.when(s[2] != 0)
        def _():
            fill((o0, o1), (g0, g1))

    def put(rows, feed, back):
        feed_out[rows] = (feed_in[rows].astype(F32) + feed).astype(BF16)
        back_out[rows] = (back_in[rows].astype(F32) + back).astype(BF16)

    hidden_part(normed[...], grad_feed[...], up, down, small[6:7].astype(F32), active_out, upper_out, bias_out, put)


def output_body(s, n, middle, feed, side, params, own_out):
    total = feed[...].astype(F32) + side[...].astype(F32)
    own_out[...] = (middle[...].astype(F32) + total + params[5:6]).astype(BF16)


def split_body(s, n, whole_in, *outs):
    count = outs[0].shape[0]
    mine = 2 * s[4] + s[5]
    for k, out in enumerate(outs):
        start = pl.multiple_of((mine ^ k) * count, 8)
        out[...] = whole_in[pl.ds(start, count)]


def second_body(s, n, *refs):
    up, down = refs[:4], refs[4:8]
    outs = refs[8:]
    for (near, got_near, away, got_away), bit, (kept, sent) in ((up, s[5], outs[:2]), (down, s[4], outs[2:])):
        count = kept.shape[1]
        for k, (own, got) in enumerate(((near, got_near), (away, got_away))):
            for target, half in ((kept, bit), (sent, 1 - bit)):
                rows = pl.ds(pl.multiple_of(half * count, 8), count)
                target[k] = (own[rows].astype(F32) + got[rows].astype(F32)).astype(BF16)


def third_body(s, n, up, got_up, down, got_down, up_out, down_out, sent):
    count = up.shape[1]
    for k, (own, got, out) in enumerate(((up, got_up, up_out), (down, got_down, down_out))):
        out[...] = (own[0].astype(F32) + got[0].astype(F32)).astype(BF16)
        sent[k * count : (k + 1) * count] = (own[1].astype(F32) + got[1].astype(F32)).astype(BF16)


def join_hidden_body(s, n, up, up_near, up_other, down, down_near, down_other, up_out, down_out):
    count = up.shape[0]
    first, second = slice(0, count), slice(count, 2 * count)
    lists = (
        (up_out, s[4], s[5], ((0, 0, up, first), (0, 1, up_near, first), (1, 0, up_other, first), (1, 1, up_other, second))),
        (down_out, s[5], s[4], ((0, 0, down, first), (0, 1, down_near, first), (1, 0, down_other, first), (1, 1, down_other, second))),
    )
    for out, high, low, pieces in lists:
        for at_high, at_low, piece, rows in pieces:
            place = 2 * (high ^ at_high) + (low ^ at_low)
            out[pl.ds(pl.multiple_of(place * count, 8), count)] = piece[rows].astype(F32)


def join_mixed_body(s, n, *refs):
    pieces, (out, query, key, value), (pair, last) = refs[:4], refs[4:8], refs[8:]
    count = pieces[0].shape[0] // 2
    group, extra = out.shape[0], out.shape[0] - LANES
    for k, piece in enumerate(pieces):
        place = 2 * (s[4] ^ (k // 2)) + (s[5] ^ (k % 2))
        rows = pl.ds(pl.multiple_of(place * count, 8), count)
        pair[rows] = piece[:count].astype(F32)
        last[rows] = piece[count:].astype(F32)
    out[...] = last[:group]
    for k, target in enumerate((query, key, value)):
        target[:LANES] = pair[k * LANES : (k + 1) * LANES]
        target[LANES:] = last[group + k * extra : group + (k + 1) * extra]


def mix_body(s, n, pair, got_pair, p0, p1, p2, p3, out):
    count = got_pair.shape[0]
    out[:count] = (pair[...].astype(F32) + got_pair[...].astype(F32)).astype(BF16)
    total = (p0[...].astype(F32) + p1[...].astype(F32)) + (p2[...].astype(F32) + p3[...].astype(F32))
    out[count:] = total.astype(BF16)


def assemble_body(places, s, n, *refs):
    pieces, result, sems = refs[: len(places)], refs[-2], refs[-1]
    copies = []
    for k, ((where, start), piece) in enumerate(zip(places, pieces)):
        target = result.at[s[3] ^ where, pl.ds(start, piece.shape[0])]
        copies.append(pltpu.make_async_copy(piece, target, sems.at[k]))
        copies[-1].start()
    for copy in copies:
        copy.wait()


def back_two_body(s, n, middle, grad_feed, g0, g1, params, w0, w1, a0, a1, branch_out, *refs):
    grad_tiles, inner_outs, sums_out = refs[:4], refs[4:8], refs[8]
    normal, inverse = normalize(middle[...].astype(F32))
    grad_normed = g0[...].astype(F32) + g1[...].astype(F32)
    grad_output = grad_feed[...].astype(F32)
    grad_middle = grad_output + norm_back(grad_normed, normal, inverse, params[2:3])
    grad_branch = grad_middle.astype(BF16)
    branch_out[...] = grad_branch
    sums = jnp.concatenate(
        [
            column_sums(grad_normed * normal),
            column_sums(grad_normed),
            column_sums(grad_branch.astype(F32)),
            column_sums(grad_output),
        ],
        0,
    )
    accumulate(sums_out, sums)
    lane = lax.broadcasted_iota(jnp.int32, (8, LANES), 1)
    head = lax.broadcasted_iota(jnp.int32, (8, LANES), 0)
    member = (lane // HEAD_DIM == head // 4).astype(BF16)
    for k, (weight, array) in enumerate(((w0, a0), (w1, a1))):
        grad_att = dot(grad_branch, weight[...], NT).astype(BF16)
        extra = grad_att.shape[1] - LANES
        gap = jnp.zeros((grad_att.shape[0], LANES - extra), BF16)
        for t in range(2):
            lanes = slice(t * LANES, (t + 1) * LANES)
            part = grad_att[:, :LANES] if t == 0 else jnp.concatenate([grad_att[:, LANES:], gap], 1)
            grad_tiles[2 * k + t][...] = part
            product = part.astype(F32) * array[:, lanes].astype(F32)
            high = product.astype(BF16)
            low = (product - high.astype(F32)).astype(BF16)
            inner_outs[2 * k + t][...] = dot(member, high, NT) + dot(member, low, NT)


def back_one_body(s, n, tokens, grad_middle, g0, g1, g2, g3, params, own_out, sums_out):
    normal, inverse = normalize(tokens[0].astype(F32))
    grad_normed = (g0[...].astype(F32) + g1[...].astype(F32)) + (g2[...].astype(F32) + g3[...].astype(F32))
    accumulate(
        sums_out, jnp.concatenate([column_sums(grad_normed * normal), column_sums(grad_normed)], 0)
    )
    back = norm_back(grad_normed, normal, inverse, params[0:1])
    own_out[...] = (grad_middle[...].astype(F32) + back).astype(BF16)


def pairs(count, mask):
    return [(i, i ^ mask) for i in range(count)]


def overlap(moves, kernel=None, inputs=()):
    operands, inputs = lax.optimization_barrier((tuple(v for _, v in moves), tuple(inputs)))
    received = tuple(move(v) for (move, _), v in zip(moves, operands))
    results = tuple(kernel(*inputs)) if kernel else ()
    return lax.optimization_barrier((received, results))


def after(value, *others):
    return lax.optimization_barrier((value, *others))[0]


def local(
    dp, tp,
    tokens, cube_lengths, query_weight, query_bias, key_weight, value_weight, value_bias,
    out_weight, out_bias, first_gain, first_shift, second_gain, second_shift,
    up_weight, up_bias, down_weight, down_bias, cotangent,
):
    slots, length, width = tokens.shape
    group = query_weight.shape[1]
    hidden = up_weight.shape[1]
    blocks = length // ROWS
    half = length // 2
    half_rows = half // 2
    mine = lax.axis_index("tp")
    place = lax.axis_index("dp")
    cube, core = mine // 2, mine % 2
    parity = place & 1
    bits = [1 << k for k in range(dp.bit_length() - 1)]
    scalars = (jnp.stack([cube, core, parity, mine, parity, (place // 2) & 1]).astype(jnp.int32), cube_lengths)

    def to_core(v):
        return lax.ppermute(v, "tp", pairs(tp, 1))

    def to_chip(v):
        return lax.ppermute(v, "tp", pairs(tp, 2))

    def to_place(v, mask):
        return lax.ppermute(v, "dp", pairs(dp, mask))

    full = (length, width)
    span = 3 * LANES
    extra = group - LANES
    vectors = whole((8, width))
    part_spec = whole((span, width))
    part_shape = shape_of((length, span), BF16)

    top = span + 3 * extra
    far_shape = (top + 16, width)
    anywhere = pl.BlockSpec(memory_space=pl.ANY)
    vector = pl.BlockSpec((width,), lambda i, s, n: (0,))
    short_vector = pl.BlockSpec((group,), lambda i, s, n: (0,))
    lead_rows = hidden // 2
    sent, third_0, params, lead, rest = run(
        pack_body, scalars, (1,),
        [anywhere] * 5 + [vector] * 7 + [short_vector] * 2,
        [whole(far_shape), part_spec, vectors, whole((lead_rows, width)), whole((hidden - lead_rows, width))],
        [shape_of(far_shape, BF16), shape_of((span, width), BF16), shape_of((8, width), F32),
         shape_of((lead_rows, width), BF16), shape_of((hidden - lead_rows, width), BF16)],
        scratch=[pltpu.SemaphoreType.DMA((12,))],
        name="pack_weights", room=10,
    )(
        *map(in_hbm, (
            query_weight.T, key_weight.T, value_weight.T, up_weight, down_weight,
            first_gain, first_shift, second_gain, second_shift, out_bias, down_bias, up_bias, query_bias, value_bias,
        ))
    )
    far = to_chip(sent)

    def spread(rows):
        gap = ((0, 0), (0, LANES - extra), (0, 0))
        return jnp.pad(rows.reshape(3, extra, width), gap).reshape(span, width)

    normed, part_0, part_1 = run(
        first_body, scalars, (blocks,),
        [cube_rows(width), vectors, part_spec, part_spec],
        [rows_of(width), rows_of(span), rows_of(span)],
        [shape_of(full, BF16), part_shape, part_shape],
        name="first_norm_project", room=10,
    )(in_hbm(tokens), params, sent, third_0)
    pair_0 = sent[:span]

    def attend(pair, third):
        step = length // 2
        query = pl.BlockSpec((step, LANES), lambda i, s, n: (i, 0))
        return run(
            attend_body, scalars, (2,),
            [query, query, whole((length, span)), whole((length, span))],
            [pl.BlockSpec((step, 2 * LANES), lambda i, s, n: (i, 0)), pl.BlockSpec((16, step), lambda i, s, n: (0, i))],
            [shape_of((length, 2 * LANES), BF16), shape_of((16, length), F32)],
            name="attend", room=14,
        )(pair, third, pair, third)

    def project(weight, bias, at):
        return scaled(dot(normed, weight, NT) + bias[:, at * span : (at + 1) * span])

    att_0, log_0 = attend(part_0, part_1)
    far = after(far, att_0)
    pair_1, third_1 = far[:span], spread(far[span:top])
    bias_1 = far[top + 7 : top + 8].astype(F32)
    part_2 = project(pair_1, bias_1, 0)
    part_3 = project(third_1, bias_1, 1)
    got_0 = to_chip(after(lead, far))
    (side_0, out_far), (att_1, log_1) = overlap([(to_core, att_0), (to_chip, out_weight)], attend, (part_2, part_3))
    out_side = to_core(jnp.concatenate([out_weight, out_far], 0))
    side_1 = to_core(att_1)

    double_tile = rows_of(2 * LANES)

    def out_block(at):
        return pl.BlockSpec((group, width), lambda i, s, n: (at, 0))

    out_specs = [out_block(0), out_block(0), out_block(0), out_block(1)]
    middle, normed_two = run(
        middle_body, scalars, (blocks,),
        [cube_rows(width), vectors] + [double_tile] * 4 + out_specs,
        [rows_of(width)] * 2,
        [hbm_shape(full, BF16), shape_of(full, BF16)],
        name="attention_out_norm", room=12,
    )(in_hbm(tokens), params, att_0, att_1, side_0, side_1, out_weight, out_far, out_side, out_side)

    own_spec = pl.BlockSpec((half_rows, width), lambda i, s, n: (s[1] * 2 + i, 0))
    plain = pl.BlockSpec((half_rows, width), lambda i, s, n: (i, 0))
    own_shape = shape_of((half, width), BF16)

    def assemble(pieces, base=None):
        bases = [] if base is None else [base]
        return run(
            partial(assemble_body, tuple(place for place, _ in pieces)), scalars, (1,),
            [whole(piece.shape) for _, piece in pieces] + [anywhere] * len(bases), [anywhere], [shape_of((tp, half, width), BF16)],
            scratch=[pltpu.SemaphoreType.DMA((len(pieces),))], alias={len(pieces): 0} if bases else None,
            name="assemble", room=12,
        )(*(piece for _, piece in pieces), *bases)[0]

    def side_half(v):
        return lax.dynamic_slice(v, ((1 - core) * half, 0), (half, v.shape[1]))

    def bit_of(mask):
        return (place // mask) & 1

    def half_at(v, bit):
        count = v.shape[-2] // 2
        return lax.dynamic_slice_in_dim(v, bit * count, count, v.ndim - 2)

    def half_out(v, mask):
        return half_at(v, 1 - bit_of(mask))

    def half_kept(v, mask):
        return half_at(v, bit_of(mask))

    def add(a, b):
        return (a.astype(F32) + b.astype(F32)).astype(BF16)

    def join(v, other, mask):
        return jnp.where(bit_of(mask) == 0, jnp.concatenate([v, other], 0), jnp.concatenate([other, v], 0))

    both = shape_of((length, hidden), BF16)
    hidden_shapes = [both, both, hbm_shape(full, BF16), shape_of(full, BF16), shape_of((1, hidden), F32)]

    hidden_specs = [rows_of(hidden), rows_of(hidden), rows_of(width), rows_of(width), whole((1, hidden))]

    own_call = run(
        hidden_own_body, scalars, (blocks,),
        [rows_of(width), cube_rows(width), whole((width, hidden)), whole((hidden, width)), vectors],
        [rows_of(width)] + hidden_specs,
        [shape_of(full, BF16)] + hidden_shapes,
        name="hidden_own", room=16,
    )
    (got_1, other_0), (grad_feed, active_0, upper_0, feed, back, up_bias_0) = overlap(
        [(to_chip, rest), (partial(to_place, mask=1), got_0)],
        own_call,
        (normed_two, in_hbm(cotangent), in_hbm(up_weight), in_hbm(down_weight), params),
    )
    other_1 = to_place(got_1, 1)

    def hidden_grads(active, upper):
        return dot(normed_two, upper, TN).astype(BF16), dot(active, grad_feed, TN).astype(BF16)

    near = hidden_grads(active_0, upper_0)
    orders = [bits, bits[1:2] + bits[:1] + bits[2:]]
    far_call = run(
        hidden_far_body, scalars, (blocks,),
        [rows_of(width)] * 4 + [anywhere] * 4 + [pl.BlockSpec((16, width), lambda i, s, n: (top // 16, 0))],
        hidden_specs,
        [hbm_shape(both.shape, BF16)] * 2 + hidden_shapes[2:],
        scratch=[pltpu.VMEM((width, hidden), BF16), pltpu.VMEM((hidden, width), BF16), pltpu.SemaphoreType.DMA((4,))],
        name="hidden_far", room=16,
    )

    square = [bits[1], bits[0], bits[0] | bits[1]]

    def quarters(v):
        piece = (v.shape[0] // 4, v.shape[1])
        return run(
            split_body, scalars, (1,), [whole(v.shape)], [whole(piece)] * 4, [shape_of(piece, BF16)] * 4, name="split", room=8
        )(v)

    def to_square(pieces):
        return [(partial(to_place, mask=mask), v) for mask, v in zip(square, pieces)]

    sent_near = [half_out(v, order[0]) for v, order in zip(near, orders)]

    def over(order, k):
        return lambda v: to_place(v, order[k])

    got_near, (active_1, upper_1, feed, back, up_bias_1) = overlap(
        [(over(order, 0), v) for v, order in zip(sent_near, orders)],
        far_call,
        (normed_two, grad_feed, feed, back, got_0, got_1, other_0, other_1, far),
    )
    side_back = to_core(back)
    side_feed = to_core(side_half(feed))
    away = hidden_grads(active_1, upper_1)
    (own_output,) = run(
        output_body, scalars, (2,),
        [own_spec] * 2 + [plain, vectors],
        [plain], [own_shape], name="output", room=8,
    )(after(middle, *away), feed, side_feed, params)
    sent_away = [half_out(v, order[0]) for v, order in zip(away, orders)]

    tile = rows_of(LANES)
    tile_shape = hbm_shape((length, LANES), BF16)
    inner_shape = hbm_shape((8, length), F32)
    two_call = run(
        back_two_body, scalars, (blocks,),
        [rows_of(width)] * 4 + [vectors] + out_specs[:2] + [double_tile] * 2,
        [rows_of(width)] + [tile] * 4 + [pl.BlockSpec((8, ROWS), lambda i, s, n: (0, i))] * 4 + [whole((4, width))],
        [hbm_shape(full, BF16)] + [tile_shape] * 4 + [inner_shape] * 4 + [shape_of((4, width), F32)],
        name="second_norm_back", room=13,
    )
    (far_output_0, side_output, *got_away), results = overlap(
        [(to_chip, own_output[:half_rows]), (to_core, own_output)] + [(over(order, 0), v) for v, order in zip(sent_away, orders)],
        two_call,
        (middle, in_hbm(grad_feed), back, side_back, params, out_weight, out_far, in_hbm(att_0), in_hbm(att_1)),
    )
    grad_branch, gt_0, gt_1, gt_2, gt_3, in_0, in_1, in_2, in_3, sums_two = results

    def attend_back(qkv, grad, logsum, inner, count):
        at = 2 - count
        return run(
            partial(attend_back_body, count), scalars, (1,),
            [whole((length, span)), whole((length, LANES)), pl.BlockSpec((8, length), lambda i, s, n: (at, 0)), whole((8, length))],
            [whole((length, span))],
            [part_shape],
            name="attend_back", room=13,
        )(qkv, grad, logsum, inner)

    def weight_grad(grads):
        return dot(grads, normed, TN).astype(BF16)

    def third_only(v):
        return v.reshape(3, LANES, width)[:, :extra].reshape(3 * extra, width)

    pair_back, third_back = partial(attend_back, count=2), partial(attend_back, count=1)
    second_half = hidden // 2
    kept_rows = [pl.BlockSpec((second_half, width), lambda i, s, n: (s[4], 0)), pl.BlockSpec((second_half, width), lambda i, s, n: (s[5], 0))]
    piece = whole((second_half, width))
    two_shape = (2, second_half // 2, width)
    up_kept, up_sent, down_kept, down_sent = run(
        second_body, scalars, (1,),
        [kept_rows[0], piece, kept_rows[0], piece, kept_rows[1], piece, kept_rows[1], piece],
        [whole(two_shape)] * 4, [shape_of(two_shape, BF16)] * 4, name="second_halving", room=12,
    )(near[0], got_near[0], away[0], got_away[0], near[1], got_near[1], away[1], got_away[1])
    sent_2 = [up_sent, down_sent]
    (far_output_1, across_output_0, *got_second), (grads_2,) = overlap(
        [(to_chip, own_output[half_rows:]), (to_core, far_output_0)] + [(over(order, 1), v) for v, order in zip(sent_2, orders)],
        pair_back,
        (part_2, gt_2, log_1, in_2),
    )
    quarter_shape = (second_half // 2, width)
    up_third, down_third, sent_3 = run(
        third_body, scalars, (1,),
        [whole(two_shape)] * 4, [whole(quarter_shape)] * 2 + [piece],
        [shape_of(quarter_shape, BF16)] * 2 + [shape_of((second_half, width), BF16)], name="third_sum", room=10,
    )(up_kept, got_second[0], down_kept, got_second[1])
    (across_output_1, got_third), (grads_0,) = overlap(
        [(to_core, far_output_1), (to_chip, sent_3)], pair_back, (part_0, gt_0, log_0, in_0)
    )
    out_grads = [dot(a, grad_branch, TN).astype(BF16)[:group] for a in (att_0, att_1)]
    quarter = got_third.shape[0] // 2
    stage_4 = [add(v, got_third[k * quarter : (k + 1) * quarter]) for k, v in enumerate((up_third, down_third))]
    pair_away = weight_grad(grads_2)
    back_most = dot(grads_2, pair_1, NN) + dot(grads_0, pair_0, NN)
    (pair_far, got_up), (grads_3,) = overlap(
        [(to_chip, pair_away), (over(bits, 2), stage_4[0])], third_back, (part_3, gt_3, log_1, in_3)
    )
    third_away = third_only(weight_grad(grads_3))
    back_most = (back_most + dot(grads_3, third_1, NN)).astype(BF16)
    side_most_sent = side_half(back_most)
    pair = add(weight_grad(grads_0), pair_far)
    sent_pair = half_out(pair, bits[0])
    last_away = jnp.concatenate([out_grads[1], third_away], 0)
    (got_pair, last_far, side_most, got_down), (grads_1,) = overlap(
        [(over(bits, 0), sent_pair), (to_chip, last_away), (to_core, side_most_sent), (over(bits, 2), stage_4[1])],
        third_back,
        (part_1, gt_1, log_0, in_1),
    )
    back_last = dot(grads_1, third_0, NN).astype(BF16)
    side_last = to_core(side_half(back_last))
    last = add(jnp.concatenate([out_grads[0], third_only(weight_grad(grads_1))], 0), last_far)
    last_pieces = quarters(last)
    pair = add(half_kept(pair, bits[0]), got_pair)
    sent_pair = half_out(pair, bits[1])
    totals = [add(v, g) for v, g in zip(stage_4, (got_up, got_down))]
    for mask in bits[3:]:
        totals = [add(v, to_place(v, mask)) for v in totals]

    token_spec = pl.BlockSpec((1, half_rows, width), lambda i, s, n: (s[0], s[1] * 2 + i, 0))
    one_call = run(
        back_one_body, scalars, (2,),
        [token_spec, own_spec, own_spec, own_spec, plain, plain, vectors],
        [plain, whole((2, width))],
        [own_shape, shape_of((2, width), F32)],
        name="first_norm_back", room=14,
    )
    (got_pair, *got_last), (own_grad, sums_one) = overlap(
        [(over(bits, 1), sent_pair)] + to_square(last_pieces[1:]),
        one_call,
        (in_hbm(tokens), in_hbm(grad_branch), back_most, back_last, side_most, side_last, params),
    )

    first_part = half // 3 // LANES * LANES
    def beside_first(own, side, far_0, far_1, across_0, across_1, *parts):
        whole_output = assemble([
            ((0, 0), own), ((1, 0), side), ((2, 0), far_0), ((2, half_rows), far_1), ((3, 0), across_0), ((3, half_rows), across_1),
        ])
        count = parts[1].shape[0]
        (mixed,) = run(
            mix_body, scalars, (1,),
            [pl.BlockSpec((count, width), lambda i, s, n: (s[5], 0))] + [whole(v.shape) for v in parts[1:]],
            [whole((2 * count, width))], [shape_of((2 * count, width), BF16)], name="mix", room=8,
        )(*parts)
        return whole_output, mixed

    (far_0, side_grad, up_near, down_near, first_sums), (output, mixed) = overlap(
        [(to_chip, own_grad[:first_part]), (to_core, own_grad)]
        + [(over(order, 1), v) for v, order in zip(totals, orders)]
        + [(to_core, sums_one)],
        beside_first,
        (own_output, side_output, far_output_0, far_output_1, across_output_0, across_output_1, pair, got_pair, last_pieces[0], *got_last),
    )
    output = output.reshape(slots, length, width)
    first_sums = sums_one + first_sums

    def bias_sums(pair, third):
        return jnp.concatenate([sum_rows(pair), sum_rows(third)], 1)

    shared = [sums_two, first_sums]
    sums = jnp.concatenate(shared + [up_bias_0, bias_sums(grads_0, grads_1)], 0)
    sums_away = jnp.concatenate(shared + [up_bias_1, bias_sums(grads_2, grads_3)], 0)
    both_up, both_down = (jnp.concatenate([v, g], 0) for v, g in zip(totals, (up_near, down_near)))
    (far_1, up_other, down_other, got_mixed, got_sums), _ = overlap(
        [(to_chip, own_grad[first_part:]), (over(bits, 0), both_up), (over(bits, 1), both_down), (over(bits, 2), mixed), (to_chip, sums_away)]
    )
    mixed = add(mixed, got_mixed)
    for mask in bits[3:]:
        mixed = add(mixed, to_place(mixed, mask))
    sums = sums + got_sums

    def beside_last(own, side, far_0, far_1, *parts):
        base = assemble([((0, 0), own), ((1, 0), side), ((2, 0), far_0), ((2, first_part), far_1)])
        shape = (hidden, width)
        hidden_grads = run(
            join_hidden_body, scalars, (1,), [whole(v.shape) for v in parts], [whole(shape)] * 2, [shape_of(shape, F32)] * 2,
            name="join_hidden", room=14,
        )(*parts)
        return base, *hidden_grads

    (*got_mixed, across_1, across_0), (base, up_total, down_total) = overlap(
        to_square([mixed] * 3) + [(to_core, far_1), (to_core, far_0)],
        beside_last,
        (own_grad, side_grad, far_0, far_1, totals[0], up_near, up_other, totals[1], down_near, down_other),
    )
    got_z, got_y, got_yz = overlap(to_square([sums] * 3))[0]
    sums = (sums + got_y) + (got_z + got_yz)
    for mask in bits[2:]:
        sums = sums + to_place(sums, mask)
    out_grad, *qkv_grads = run(
        join_mixed_body, scalars, (1,), [whole(mixed.shape)] * 4, [whole((group, width))] * 4, [shape_of((group, width), F32)] * 4,
        scratch=[pltpu.VMEM((2 * group, width), F32)] * 2, name="join_mixed", room=12,
    )(mixed, *got_mixed)
    input_grad = assemble([((3, 0), across_0), ((3, first_part), across_1)], base).reshape(slots, length, width)

    def bias_of(k):
        start = k * LANES
        return jnp.concatenate([sums[7, start : start + LANES], sums[7, span + start : span + start + extra]])

    return (
        output,
        input_grad,
        qkv_grads[0].T,
        bias_of(0),
        qkv_grads[1].T,
        qkv_grads[2].T,
        bias_of(2),
        out_grad,
        sums[2],
        sums[4],
        sums[5],
        sums[0],
        sums[1],
        up_total,
        sums[6],
        down_total,
        sums[3],
    )


def solution(mesh):
    dp, tp = mesh.shape["dp"], mesh.shape["tp"]
    placed = (
        P("dp", None, None),
        P("dp"),
        P(None, "tp"),
        P("tp"),
        P(None, "tp"),
        P(None, "tp"),
        P("tp"),
        P("tp", None),
        P(),
        P(),
        P(),
        P(),
        P(),
        P(None, "tp"),
        P("tp"),
        P("tp", None),
        P(),
        P("dp", None, None),
    )
    return jax.shard_map(
        partial(local, dp, tp),
        mesh=mesh,
        in_specs=placed,
        out_specs=(
            P("dp", None, None),
            P("dp", None, None),
            P(None, "tp"),
            P("tp"),
            P(None, "tp"),
            P(None, "tp"),
            P("tp"),
            P("tp", None),
            P(),
            P(),
            P(),
            P(),
            P(),
            P(None, "tp"),
            P("tp"),
            P("tp", None),
            P(),
        ),
        check_vma=False,
    )
```
